32 devices in a mesh: seq: 2 (over y), wt: 4 (over x, core), grp: 4 (over z).
Axes of the slice: x: 2, y: 2, z: 4, core: 2. Of those that a mesh axis runs over, the one named last changes fastest.
Arguments:
- tokens: bfloat16 [4, 2048, 2048], P('grp', ('seq', 'wt')), may hold values from -6 to 6
- lengths: int32 [4, 4], P('grp'), may hold values from 1 to 1025, 2048 in all within a row
- order: int32 [4, 2048], P('grp'), may hold values from 0 to 2047, as said below
- mixer_gain: float32 [2048], replicated, may hold values from 0.1 to 1.9
- feed_gain: float32 [2048], replicated, may hold values from 0.1 to 1.9
- in_weight: bfloat16 [2048, 3, 2048], P(('seq', 'grp'), None, 'wt'), may hold values from -0.125 to 0.125
- conv_taps: bfloat16 [3, 2048], P(None, 'wt'), may hold values from -3.5 to 3.5
- out_weight: bfloat16 [2048, 2048], P('wt', ('seq', 'grp')), may hold values from -0.125 to 0.125
- gate_up: bfloat16 [2048, 2, 8192], P(('seq', 'grp'), None, 'wt'), may hold values from -0.125 to 0.125
- down_weight: bfloat16 [8192, 2048], P('wt', ('seq', 'grp')), may hold values from -0.0625 to 0.0625
- cotangent: bfloat16 [4, 2048, 2048], P('grp', ('seq', 'wt')), may hold values from -6 to 6
Outputs:
- block_out: bfloat16 [4, 2048, 2048], P('grp', ('seq', 'wt'))
- tokens_grad: float32 [4, 2048, 2048], P('grp', ('seq', 'wt'))
- mixer_grad: float32 [2048], replicated
- feed_grad: float32 [2048], replicated
- in_grad: float32 [2048, 3, 2048], P(('seq', 'grp'), None, 'wt')
- taps_grad: float32 [3, 2048], P(None, 'wt')
- out_grad: float32 [2048, 2048], P('wt', ('seq', 'grp'))
- gating_grad: float32 [2048, 2, 8192], P(('seq', 'grp'), None, 'wt')
- down_grad: float32 [8192, 2048], P('wt', ('seq', 'grp'))
The draws below stay inside these ranges and needn't reach their ends.
Inputs may be any that keep to these rules, and one draw needn't show every extreme that they name: The 4 lengths of each sequence sum to 2048, and the longest is exactly 1025. Each row of order is a permutation of the 2048 positions. Split the slots and the positions alike into aligned blocks of 256; every block of slots holds exactly 32 positions of every block of positions.
All inputs are finite; a program needn't handle non-finite values.
Results may differ from the reference program's by a relative error of at most 0.015.
Values may be sent and summed in bfloat16 or wider, within the bound.
No kernel may reach another device: no remote copies, remote signals or barrier semaphores. Data moves between devices by JAX's collectives and lax.ppermute only.
A program may use at most 256 MiB of HBM per device.

```python
import math
import jax
import jax.numpy as jnp
import numpy as np
from jax import lax

D = 2048
FF = 8192
KERNEL = 3
ROWS = 256
NDOC = 4
SPAN = 1024
LEN = 2048
SEQS = 4
N_SEQ = 2
N_WT = 4


def draw_order(key, part):
    groups = N_SEQ * N_WT
    per_peer = ROWS // groups

    def one_home(home_key, home_index):
        return home_index * ROWS + jax.random.permutation(home_key, ROWS).astype(jnp.int32)

    def shuffle_slots(slot_key, slot_row):
        return slot_row[jax.random.permutation(slot_key, ROWS)]

    def one_sequence(seq_key):
        home_keys = jax.random.split(jax.random.fold_in(seq_key, 1), groups)
        dealt_rows = jax.vmap(one_home)(home_keys, jnp.arange(groups, dtype=jnp.int32))
        dealt_rows = dealt_rows.reshape(groups, groups, per_peer).transpose(1, 0, 2).reshape(groups, ROWS)
        slot_keys = jax.random.split(jax.random.fold_in(seq_key, 2), groups)
        shuffled = jax.vmap(shuffle_slots)(slot_keys, dealt_rows)
        return shuffled.reshape(groups * ROWS).astype(jnp.int32)
    return jax.vmap(one_sequence)(jax.random.split(jax.random.fold_in(key, 7), SEQS))


def block_levels(stream_key, dims, shards, low, largest):
    level, own = 1.0, jax.random.fold_in(stream_key, 6)
    for axis_at, shards_of in shards:
        steps = jnp.exp(jax.random.uniform(jax.random.fold_in(own, axis_at), (shards_of,), jnp.float32, low / len(shards), largest / len(shards)))
        level = level * jnp.repeat(steps, dims[axis_at] // shards_of).reshape([-1 if axis == axis_at else 1 for axis in range(len(dims))])
    return level


def split_up(count, total, limit, slope):
    weights = [(1 << 20) // math.isqrt(rank ** slope) + 1 for rank in range(2, count + 1)]
    spare, counts = total - limit - (count - 1), [1] * (count - 1)
    while spare > 0:
        free = [i for i in range(count - 1) if counts[i] < limit]
        whole, left = sum([weights[i] for i in free]), spare
        for i in free:
            more = min(limit - counts[i], max(1, left * weights[i] // whole), spare)
            counts[i] = counts[i] + more
            spare = spare - more
    return np.array([limit] + counts)


def uneven_parts(own_key, count, total, limit, lean):
    if count == 2:
        one = jax.random.randint(own_key, (), max(1, total - limit), min(limit, total - 1) + 1)
        return jnp.stack([one, total - one])
    sizes = jnp.asarray(split_up(count, total, limit, lean), jnp.int32)
    twos = (count - 1) // 2
    donor, taker = sizes[1:1 + 2 * twos:2], sizes[2:2 + 2 * twos:2]
    slack = jnp.minimum(donor - 1, limit - taker)
    moved = jax.random.randint(jax.random.fold_in(own_key, 1), (twos,), 0, 1 << 20) % (slack + 1)
    sizes = sizes.at[1:1 + 2 * twos:2].set(donor - moved).at[2:2 + 2 * twos:2].set(taker + moved)
    return sizes[jax.random.permutation(jax.random.fold_in(own_key, 2), count)]


def gaussian(rng, shape, spread, reach, cuts=(), kind=jnp.bfloat16):
    values = spread * jax.random.normal(rng, shape, jnp.float32)
    if cuts:
        values = values * block_levels(rng, shape, cuts, -0.22, 0.18)
    return jnp.clip(values, -reach, reach).astype(kind)


def setup_inputs(seed: int = 0) -> dict:
    key_of = jax.random.split(jax.random.key(seed), 12)
    tokens = gaussian(key_of[0], (SEQS, LEN, D), 1.0, 6.0, ((0, 4), (1, 8)))
    lengths = jax.vmap(lambda own: uneven_parts(own, NDOC, LEN, LEN - SPAN + 1, 0))(jax.random.split(key_of[1], SEQS)).reshape((SEQS, NDOC)).astype(jnp.int32)
    order = draw_order(jax.random.fold_in(key_of[11], 71), 0)
    mixer_gain = jnp.clip(1.0 + 0.18 * jax.random.normal(key_of[3], (D,), jnp.float32), 0.1, 1.9)
    feed_gain = jnp.clip(1.0 + 0.18 * jax.random.normal(key_of[4], (D,), jnp.float32), 0.1, 1.9)
    in_weight = gaussian(key_of[5], (D, 3, D), D ** -0.5, 0.125, ((0, 8), (2, 4)))
    conv_taps = gaussian(key_of[6], (KERNEL, D), KERNEL ** -0.5, 3.5, ((1, 4),))
    out_weight = gaussian(key_of[7], (D, D), D ** -0.5, 0.125, ((0, 4), (1, 8)))
    gate_up = gaussian(key_of[8], (D, 2, FF), D ** -0.5, 0.125, ((0, 8), (2, 4)))
    down_weight = gaussian(key_of[9], (FF, D), FF ** -0.5, 0.0625, ((0, 4), (1, 8)))
    cotangent = gaussian(key_of[10], (SEQS, LEN, D), 1.0, 6.0, ((0, 4), (1, 8)))
    return dict(tokens=tokens, lengths=lengths, order=order, mixer_gain=mixer_gain, feed_gain=feed_gain, in_weight=in_weight, conv_taps=conv_taps, out_weight=out_weight, gate_up=gate_up, down_weight=down_weight, cotangent=cotangent)


epsilon = 1e-05
highest = lax.Precision.HIGHEST

@jax.custom_vjp
def low(v):
    return lax.optimization_barrier(v.astype(jnp.bfloat16)).astype(jnp.float32)

@jax.custom_vjp
def low_back(v):
    return v

def low_keep(v):
    return (low(v), None)

def low_pass(kept, grad):
    return (grad,)

def back_keep(v):
    return (v, None)

def back_low(kept, grad):
    return (low(grad),)
low.defvjp(low_keep, low_pass)
low_back.defvjp(back_keep, back_low)

def rms_scale(values):
    return lax.rsqrt(lax.optimization_barrier(jnp.mean(values * values, axis=-1, keepdims=True)) + epsilon)

def conv_masks(lengths_row, count):
    positions = jnp.arange(count, dtype=jnp.int32)
    starts = (jnp.cumsum(lengths_row) - lengths_row).astype(jnp.int32)
    opening = lax.optimization_barrier(jnp.max(jnp.where(starts[None, :] <= positions[:, None], starts[None, :], 0), axis=1))
    mask_one = (positions - 1 >= opening).astype(jnp.float32)[:, None]
    mask_two = (positions - 2 >= opening).astype(jnp.float32)[:, None]
    return (mask_one, mask_two)

def block_forward(token_rows, mixer_gain, feed_gain, in_weight, conv_taps, out_weight, gate_up, down_weight, mask_one, mask_two):
    normed = low(token_rows * rms_scale(token_rows) * mixer_gain)
    projected = low_back(jnp.einsum('td,dkc->tkc', normed, in_weight, precision=highest))
    in_gate = projected[:, 0]
    out_gate = projected[:, 1]
    values = projected[:, 2]
    gated = low(low_back(in_gate * values))
    shift_one = jnp.pad(gated, ((1, 0), (0, 0)))[:-1]
    shift_two = jnp.pad(gated, ((2, 0), (0, 0)))[:-2]
    mixed = low_back(conv_taps[2] * gated + mask_one * conv_taps[1] * shift_one + mask_two * conv_taps[0] * shift_two)
    mixed_out = low(out_gate * mixed)
    branch = low_back(jnp.dot(mixed_out, out_weight, precision=highest))
    hidden_state = token_rows + branch
    feed_in = low(hidden_state * rms_scale(hidden_state) * feed_gain)
    gates = low_back(jnp.einsum('td,dkf->tkf', feed_in, gate_up, precision=highest))
    activated = low(jax.nn.silu(gates[:, 0]) * gates[:, 1])
    feed_out = low_back(jnp.dot(activated, down_weight, precision=highest))
    return hidden_state + feed_out

def reference(tokens, lengths, order, mixer_gain, feed_gain, in_weight, conv_taps, out_weight, gate_up, down_weight, cotangent):
    params = (mixer_gain.astype(jnp.float32), feed_gain.astype(jnp.float32), in_weight.astype(jnp.float32), conv_taps.astype(jnp.float32), out_weight.astype(jnp.float32), gate_up.astype(jnp.float32), down_weight.astype(jnp.float32))

    def one_sequence(totals, inputs):
        row_tokens, row_lengths, row_order, row_cotangent = inputs
        inverse = jnp.argsort(row_order).astype(jnp.int32)
        home_tokens = row_tokens[inverse]
        home_cotangent = row_cotangent[inverse]
        mask_one, mask_two = conv_masks(row_lengths, LEN)

        def forward(row_in, gain_one, gain_two, weight_in, taps, weight_out, weight_gate, weight_down):
            return block_forward(row_in, gain_one, gain_two, weight_in, taps, weight_out, weight_gate, weight_down, mask_one, mask_two)
        result, pullback = jax.vjp(forward, home_tokens.astype(jnp.float32), *params)
        grads = pullback(home_cotangent.astype(jnp.float32))
        updated = tuple((running + update for running, update in zip(totals, grads[1:])))
        return (updated, (result.astype(jnp.bfloat16)[row_order], grads[0][row_order]))
    zeros = tuple((jnp.zeros_like(weight_item) for weight_item in params))
    totals, stacked = lax.scan(one_sequence, zeros, (tokens, lengths, order, cotangent))
    return (stacked[0], stacked[1], totals[0], totals[1], totals[2], totals[3], totals[4], totals[5], totals[6])
```

```python
import jax
import jax.numpy as jnp
from jax import lax
from jax.sharding import PartitionSpec as P

epsilon = 1e-05
bf16 = jnp.bfloat16
f32 = jnp.float32
contract_rows = (((0,), (0,)), ((), ()))
contract_cols = (((1,), (1,)), ((), ()))


def rotated(array, axis, by):
    count = lax.axis_size(axis)
    return lax.ppermute(array, axis, [(i, (i + by) % count) for i in range(count)])


def crossed(array, axis, by):
    count = lax.axis_size(axis)
    return lax.ppermute(array, axis, [(i, i ^ by) for i in range(count)])


def passed_along(array, axis, by):
    count = lax.axis_size(axis)
    pairs = [(i, i + by) for i in range(count) if 0 <= i + by < count]
    return lax.ppermute(array, axis, pairs)


class Chain:
    def __init__(self, depth):
        self.depth = depth
        self.arrived = []

    def send(self, array, move):
        if len(self.arrived) >= self.depth:
            array, _ = lax.optimization_barrier((array, self.arrived[-self.depth]))
        result = move(array)
        self.arrived.append(result)
        return result


def rms_scale(values):
    return lax.rsqrt(jnp.mean(values * values, axis=-1, keepdims=True) + epsilon)


def relative_columns(array, seq_at, grp_at, seq_count, grp_count):
    width = array.shape[1] // (seq_count * grp_count)
    blocks = {
        (a, b): array[:, (a * grp_count + b) * width : (a * grp_count + b + 1) * width]
        for a in range(seq_count)
        for b in range(grp_count)
    }
    blocks = {(a, b): blocks[(-a % seq_count, -b % grp_count)] for a, b in blocks}
    step = 1
    while step < seq_count:
        chosen = (seq_at // step) % 2 == 1
        blocks = {
            (a, b): jnp.where(chosen, blocks[((a - step) % seq_count, b)], blocks[(a, b)])
            for a, b in blocks
        }
        step *= 2
    step = 1
    while step < grp_count:
        chosen = (grp_at // step) % 2 == 1
        blocks = {
            (a, b): jnp.where(chosen, blocks[(a, (b - step) % grp_count)], blocks[(a, b)])
            for a, b in blocks
        }
        step *= 2
    return jnp.concatenate(
        [blocks[(a, b)] for a in range(seq_count) for b in range(grp_count)], axis=1
    )


def gather_rows(values):
    count = lax.axis_size("wt")
    blocks = {0: values}
    step = count // 2
    while step:
        for j in list(blocks):
            blocks[j ^ step] = crossed(blocks[j], "wt", step)
        step //= 2
    return jnp.concatenate([blocks[j] for j in range(count)], axis=0)


def scatter_rows(product):
    count = lax.axis_size("wt")
    blocks = {j: product(j) for j in sorted(range(count), key=lambda j: -(j % 2))}
    step = 1
    while step < count:
        for j in [j for j in blocks if j & step]:
            sent = blocks.pop(j).astype(bf16)
            blocks[j ^ step] = blocks[j ^ step] + crossed(sent, "wt", step).astype(f32)
        step *= 2
    return blocks[0]


def exchange(rows, peers):
    size = rows.shape[0] // peers
    parts = [rows[k * size : (k + 1) * size] for k in range(peers)]
    return jnp.concatenate(
        [parts[0]] + [crossed_both(parts[k], k, peers) for k in range(1, peers)], axis=0
    )


def crossed_both(array, by, peers):
    return lax.ppermute(array, ("seq", "wt"), [(i, i ^ by) for i in range(peers)])


def summed(array, axes):
    for axis in axes:
        step = 1
        while step < lax.axis_size(axis):
            array = array + crossed(array, axis, step)
            step *= 2
    return array


def select_rows(matrix, rows, dims):
    return lax.dot_general(matrix, rows, dims, preferred_element_type=f32).astype(bf16)


def matmul(left, right, dims=(((1,), (0,)), ((), ()))):
    return lax.dot_general(left, right, dims, preferred_element_type=f32)


def shards(
    tokens,
    lengths,
    order,
    mixer_gain,
    feed_gain,
    in_weight,
    conv_taps,
    out_weight,
    gate_up,
    down_weight,
    cotangent,
):
    local_rows = tokens.shape[1]
    seq_count, wt_count, grp_count = (lax.axis_size(a) for a in ("seq", "wt", "grp"))
    seq_at, wt_at, grp_at = (lax.axis_index(a) for a in ("seq", "wt", "grp"))
    peers = seq_count * wt_count
    per_peer = local_rows // peers
    block_index = seq_at * wt_count + wt_at
    places = [(a, b) for a in range(seq_count) for b in range(grp_count)]
    ring = list(range(1, grp_count)) + [0]

    def relative(array):
        return relative_columns(array, seq_at, grp_at, seq_count, grp_count)

    chain_seq, chain_grp = Chain(2), Chain(2)

    def gathered(pieces):
        held = [{(0, 0): piece} for piece in pieces]
        for b in range(grp_count):
            for i in range(len(pieces)):
                if b:
                    held[i][(0, b)] = chain_grp.send(
                        held[i][(0, b - 1)], lambda v: rotated(v, "grp", 1)
                    )
            for i in range(len(pieces)):
                for a in range(1, seq_count):
                    held[i][(a, b)] = chain_seq.send(
                        held[i][(0, b)], lambda v, a=a: rotated(v, "seq", a)
                    )
        return held

    down_half = down_weight.shape[0] // 2
    in_planes = [in_weight[:, k] for k in range(3)]
    in_held = gathered([jnp.stack(in_planes)])[0]
    out_held = gathered([out_weight])[0]
    gate_held = gathered([gate_up[:, k] for k in range(2)])
    down_held = gathered([down_weight[:down_half], down_weight[down_half:]])
    full_in = jnp.concatenate([in_held[p] for p in places], axis=1)
    full_out = jnp.concatenate([out_held[p] for p in places], axis=1)
    full_gate = [jnp.concatenate([h[p] for p in places], axis=0) for h in gate_held]
    full_down = [jnp.concatenate([h[p] for p in places], axis=1) for h in down_held]

    order_row = order[0]
    slot_blocks = order_row.reshape(peers, local_rows)
    here_positions = lax.dynamic_index_in_dim(slot_blocks, block_index, 0, keepdims=False)
    targets = here_positions // local_rows
    slots = jnp.arange(local_rows, dtype=jnp.int32)
    earlier = slots[:, None] < slots[None, :]
    same = (targets[:, None] == targets[None, :]) & earlier
    rank = jnp.sum(same.astype(jnp.int32), axis=0)
    send_place = (targets ^ block_index) * per_peer + rank
    send_matrix = (slots[:, None] == send_place[None, :]).astype(bf16)
    mine = slot_blocks // local_rows == block_index
    mine_rank = matmul(mine.astype(bf16), earlier.astype(bf16)).astype(jnp.int32)
    sources = jnp.arange(peers, dtype=jnp.int32) ^ block_index
    arrival = jnp.where(mine, sources[:, None] * per_peer + mine_rank, -1).reshape(-1)
    home_place = order_row - block_index * local_rows
    home_hot = (home_place[:, None] == slots[None, :]).astype(bf16)
    arrival_hot = (arrival[:, None] == slots[None, :]).astype(bf16)
    home_matrix = matmul(home_hot, arrival_hot, contract_rows).astype(bf16)
    plain = (((1,), (0,)), ((), ()))

    def to_home(rows):
        got = exchange(select_rows(send_matrix, rows, plain), peers)
        return relative(select_rows(home_matrix, got, plain))

    def to_arrival(rows):
        back = exchange(select_rows(home_matrix, relative(rows), contract_rows), peers)
        return select_rows(send_matrix, back, contract_rows)

    token_rows = to_home(tokens[0]).astype(f32)
    cot_rows = to_home(cotangent[0])
    mixer_row = relative(mixer_gain[None])
    feed_row = relative(feed_gain[None])

    scale_mix = rms_scale(token_rows)
    normed_all = gather_rows((token_rows * scale_mix * mixer_row).astype(bf16))
    span_rows = normed_all.shape[0]
    channels = out_weight.shape[0]
    in_gate, out_gate, values = (matmul(normed_all, full_in[k]) for k in range(3))
    gated = (in_gate * values).astype(bf16)

    block_at = [wt_at ^ j for j in range(wt_count)]
    tails = gated.reshape(wt_count, local_rows, channels)[:, -2:]
    carried = passed_along(
        lax.dynamic_index_in_dim(tails, wt_at ^ (wt_count - 1), 0, keepdims=False), "seq", 1
    )
    tails = jnp.concatenate([tails, carried[None]], axis=0)
    before = jnp.stack(
        [
            lax.dynamic_index_in_dim(
                tails, jnp.where(at == 0, wt_count, wt_at ^ (at - 1)), 0, keepdims=False
            )
            for at in block_at
        ]
    )
    extended = jnp.concatenate(
        [before, gated.reshape(wt_count, local_rows, channels)], axis=1
    ).astype(f32)
    positions = (
        (seq_at * wt_count + jnp.stack(block_at))[:, None] * local_rows + slots[None, :]
    )[:, :, None]
    docs = lengths.shape[1]
    starts = [sum([lengths[0, i] for i in range(d)], jnp.int32(0)) for d in range(docs)]

    def mask(at, back):
        opening = jnp.zeros_like(at)
        for start in starts:
            opening = jnp.where(start <= at, jnp.maximum(opening, start), opening)
        return (at - back >= opening).astype(f32)

    mask_one, mask_two = mask(positions, 1), mask(positions, 2)
    taps = conv_taps.astype(f32)
    now, one_back, two_back = extended[:, 2:], extended[:, 1:-1], extended[:, :-2]
    mixed = (taps[2] * now + mask_one * taps[1] * one_back + mask_two * taps[0] * two_back).reshape(
        span_rows, channels
    )
    mixed_out = (out_gate * mixed).astype(bf16)

    def rows_of(array, j):
        return array[j * local_rows : (j + 1) * local_rows]

    branch = scatter_rows(lambda j: matmul(rows_of(mixed_out, j), full_out))
    hidden_state = token_rows + branch
    scale_feed = rms_scale(hidden_state)
    feed_all = gather_rows((hidden_state * scale_feed * feed_row).astype(bf16))
    gate_part, up_part = (matmul(feed_all, full_gate[k]) for k in range(2))
    sigmoid_gate = jax.nn.sigmoid(gate_part)
    silu_gate = gate_part * sigmoid_gate
    activated = (silu_gate * up_part).astype(bf16)
    act_halves = [activated[:, :down_half], activated[:, down_half:]]
    feed_out = scatter_rows(
        lambda j: sum(matmul(rows_of(act_halves[h], j), full_down[h]) for h in range(2))
    )
    block_out = to_arrival((hidden_state + feed_out).astype(bf16))

    def reduced(terms):
        sums = [{} for _ in terms]
        for b in ring:
            for i, term in enumerate(terms):
                got = [
                    chain_seq.send(term((a, b)), lambda v, a=a: rotated(v, "seq", -a))
                    for a in range(1, seq_count)
                ]
                total = term((0, b)).astype(f32)
                for other in got:
                    total = total + other.astype(f32)
                sums[i][b] = total
        results = [s[ring[0]] for s in sums]
        for b in ring[1:]:
            for i in range(len(terms)):
                results[i] = sums[i][b] + chain_grp.send(
                    results[i].astype(bf16), lambda v: rotated(v, "grp", 1)
                ).astype(f32)
        return results

    cot_all = gather_rows(cot_rows)
    width = cot_all.shape[1] // len(places)

    def columns(array, place):
        at = (place[0] * grp_count + place[1]) * width
        return array[:, at : at + width]

    down_grad = jnp.concatenate(
        reduced(
            [
                lambda p, h=h: matmul(act_halves[h], columns(cot_all, p), contract_rows).astype(bf16)
                for h in range(2)
            ]
        ),
        axis=0,
    )
    act_grad = jnp.concatenate(
        [matmul(cot_all, full_down[h], contract_cols) for h in range(2)], axis=1
    )
    gates_grad = [
        (act_grad * up_part * sigmoid_gate * (1.0 + gate_part * (1.0 - sigmoid_gate))).astype(bf16),
        (act_grad * silu_gate).astype(bf16),
    ]
    feed_norm_grad = scatter_rows(
        lambda j: sum(
            matmul(rows_of(gates_grad[k], j), full_gate[k], contract_cols) for k in range(2)
        )
    )
    gating_grad = jnp.stack(
        reduced(
            [
                lambda p, k=k: matmul(columns(feed_all, p), gates_grad[k], contract_rows).astype(bf16)
                for k in range(2)
            ]
        ),
        axis=1,
    )
    feed_hat = hidden_state * scale_feed
    feed_term = jnp.sum(feed_norm_grad * feed_hat, axis=0)
    feed_scaled = feed_norm_grad * feed_row
    hidden_grad = cot_rows.astype(f32) + scale_feed * (
        feed_scaled - feed_hat * jnp.mean(feed_scaled * feed_hat, axis=-1, keepdims=True)
    )
    branch_grad = gather_rows(hidden_grad.astype(bf16))
    [out_grad] = reduced(
        [lambda p: matmul(mixed_out, columns(branch_grad, p), contract_rows).astype(bf16)]
    )
    mixed_out_grad = matmul(branch_grad, full_out, contract_cols)
    out_gate_grad = (mixed_out_grad * mixed).astype(bf16)
    mixed_grad = (mixed_out_grad * out_gate).astype(bf16)
    heads = mixed_grad.reshape(wt_count, local_rows, channels)[:, :2]
    incoming = passed_along(
        lax.dynamic_index_in_dim(heads, wt_at, 0, keepdims=False), "seq", -1
    )
    heads = jnp.concatenate([heads, incoming[None]], axis=0)
    after = jnp.stack(
        [
            lax.dynamic_index_in_dim(
                heads,
                jnp.where(at == wt_count - 1, wt_count, wt_at ^ (at + 1)),
                0,
                keepdims=False,
            )
            for at in block_at
        ]
    )
    grad_ext = jnp.concatenate(
        [mixed_grad.reshape(wt_count, local_rows, channels), after], axis=1
    ).astype(f32)
    mixed_low = grad_ext[:, :-2]
    gated_grad = (
        taps[2] * mixed_low
        + taps[1] * mask(positions + 1, 1) * grad_ext[:, 1:-1]
        + taps[0] * mask(positions + 2, 2) * grad_ext[:, 2:]
    )
    taps_term = jnp.stack(
        [
            jnp.sum(mixed_low * mask_two * two_back, axis=(0, 1)),
            jnp.sum(mixed_low * mask_one * one_back, axis=(0, 1)),
            jnp.sum(mixed_low * now, axis=(0, 1)),
        ]
    )
    gated_low = gated_grad.astype(bf16).astype(f32).reshape(span_rows, channels)
    projected_grad = [
        (gated_low * values).astype(bf16),
        out_gate_grad,
        (gated_low * in_gate).astype(bf16),
    ]
    [in_planes_grad] = reduced(
        [
            lambda p: jnp.stack(
                [matmul(columns(normed_all, p), g, contract_rows).astype(bf16) for g in projected_grad]
            )
        ]
    )
    in_grad = jnp.stack([in_planes_grad[k] for k in range(3)], axis=1)
    mix_norm_grad = scatter_rows(
        lambda j: sum(
            matmul(rows_of(projected_grad[k], j), full_in[k], contract_cols) for k in range(3)
        )
    )
    mix_hat = token_rows * scale_mix
    mixer_term = jnp.sum(mix_norm_grad * mix_hat, axis=0)
    mix_scaled = mix_norm_grad * mixer_row
    grad_home = hidden_grad + scale_mix * (
        mix_scaled - mix_hat * jnp.mean(mix_scaled * mix_hat, axis=-1, keepdims=True)
    )
    tokens_grad = to_arrival(grad_home.astype(bf16)).astype(f32)
    gains = summed(relative(jnp.stack([mixer_term, feed_term])), ("wt", "seq", "grp"))
    taps_grad = summed(taps_term, ("seq", "grp"))
    return (
        block_out[None],
        tokens_grad[None],
        gains[0],
        gains[1],
        in_grad,
        taps_grad,
        out_grad,
        gating_grad,
        down_grad,
    )


def solution(mesh):
    in_specs = (
        P("grp", ("seq", "wt"), None),
        P("grp", None),
        P("grp", None),
        P(),
        P(),
        P(("seq", "grp"), None, "wt"),
        P(None, "wt"),
        P("wt", ("seq", "grp")),
        P(("seq", "grp"), None, "wt"),
        P("wt", ("seq", "grp")),
        P("grp", ("seq", "wt"), None),
    )
    out_specs = (
        P("grp", ("seq", "wt"), None),
        P("grp", ("seq", "wt"), None),
        P(),
        P(),
        P(("seq", "grp"), None, "wt"),
        P(None, "wt"),
        P("wt", ("seq", "grp")),
        P(("seq", "grp"), None, "wt"),
        P("wt", ("seq", "grp")),
    )
    return jax.shard_map(shards, mesh=mesh, in_specs=in_specs, out_specs=out_specs, check_vma=False)
```

```python
import jax
import jax.numpy as jnp
from jax import lax
from jax.sharding import PartitionSpec as P

epsilon = 1e-05
bf16 = jnp.bfloat16
f32 = jnp.float32
plain = (((1,), (0,)), ((), ()))
contract_rows = (((0,), (0,)), ((), ()))
contract_cols = (((1,), (1,)), ((), ()))


def rotated(array, axis, by):
    count = lax.axis_size(axis)
    return lax.ppermute(array, axis, [(i, (i + by) % count) for i in range(count)])


def crossed(array, axis, by):
    count = lax.axis_size(axis)
    return lax.ppermute(array, axis, [(i, i ^ by) for i in range(count)])


def passed_along(array, axis, by):
    count = lax.axis_size(axis)
    pairs = [(i, i + by) for i in range(count) if 0 <= i + by < count]
    return lax.ppermute(array, axis, pairs)


def after(array, *others):
    return lax.optimization_barrier((array, *others))[0]


class Sequence:
    def __init__(self):
        self.last = ()

    def tie(self, array, *others):
        return after(array, *self.last, *others) if self.last or others else array

    def mark(self, array):
        self.last = (array,)
        return array

    def send(self, array, move, *others):
        return move(self.mark(self.tie(array, *others)))


class Chain:
    def __init__(self, stages, axis, depth):
        self.stages, self.axis, self.depth = stages, axis, depth
        self.arrived = []

    def send(self, array, by):
        behind = self.arrived[-self.depth : len(self.arrived) - self.depth + 1]
        result = self.stages.send(array, lambda v: rotated(v, self.axis, by), *behind)
        self.arrived.append(result)
        return result


def go(steps, count=1):
    for _ in range(count):
        next(steps, None)


def rest(*all_steps):
    for steps in all_steps:
        for _ in steps:
            pass


def rms_scale(values):
    return lax.rsqrt(jnp.mean(values * values, axis=-1, keepdims=True) + epsilon)


def relative_columns(array, seq_at, grp_at, seq_count, grp_count):
    width = array.shape[1] // (seq_count * grp_count)
    blocks = {
        (a, b): array[:, (a * grp_count + b) * width : (a * grp_count + b + 1) * width]
        for a in range(seq_count)
        for b in range(grp_count)
    }
    blocks = {(a, b): blocks[(-a % seq_count, -b % grp_count)] for a, b in blocks}
    step = 1
    while step < seq_count:
        chosen = (seq_at // step) % 2 == 1
        blocks = {
            (a, b): jnp.where(chosen, blocks[((a - step) % seq_count, b)], blocks[(a, b)])
            for a, b in blocks
        }
        step *= 2
    step = 1
    while step < grp_count:
        chosen = (grp_at // step) % 2 == 1
        blocks = {
            (a, b): jnp.where(chosen, blocks[(a, (b - step) % grp_count)], blocks[(a, b)])
            for a, b in blocks
        }
        step *= 2
    return jnp.concatenate(
        [blocks[(a, b)] for a in range(seq_count) for b in range(grp_count)], axis=1
    )


def peer_order(count):
    order, step = [0], count // 2
    while step:
        order = order + [j ^ step for j in order]
        step //= 2
    return order


def summed(array, axes):
    for axis in axes:
        step = 1
        while step < lax.axis_size(axis):
            array = array + crossed(array, axis, step)
            step *= 2
    return array


def select_rows(matrix, rows, dims):
    return lax.dot_general(matrix, rows, dims, preferred_element_type=f32).astype(bf16)


def matmul(left, right, dims=plain):
    return lax.dot_general(left, right, dims, preferred_element_type=f32)


def shards(
    tokens,
    lengths,
    order,
    mixer_gain,
    feed_gain,
    in_weight,
    conv_taps,
    out_weight,
    gate_up,
    down_weight,
    cotangent,
):
    local_rows = tokens.shape[1]
    seq_count, wt_count, grp_count = (lax.axis_size(a) for a in ("seq", "wt", "grp"))
    seq_at, wt_at, grp_at = (lax.axis_index(a) for a in ("seq", "wt", "grp"))
    peers = seq_count * wt_count
    per_peer = local_rows // peers
    block_index = seq_at * wt_count + wt_at
    places = [(a, b) for a in range(seq_count) for b in range(grp_count)]
    others = range(1, seq_count)
    steps = range(1, grp_count)
    ring = list(steps) + [0]
    shard_width = in_weight.shape[0]
    channels = out_weight.shape[0]
    half = gate_up.shape[2] // 2

    def relative(array):
        return relative_columns(array, seq_at, grp_at, seq_count, grp_count)

    stages = Sequence()
    by_seq, by_grp = Chain(stages, "seq", 2), Chain(stages, "grp", 2)
    backwards = [*others, 0]

    def grp_steps(held, sides=(0,)):
        for b in steps:
            for a in sides:
                held[(a, b)] = by_grp.send(held[(a, b - 1)], 1)
                yield

    def seq_steps(held, at=None):
        for b in [0, *steps] if at is None else at:
            for a in others:
                held[(a, b)] = by_seq.send(held[(0, b)], a)
            yield

    def gathering(values):
        step = wt_count // 2
        while step:
            got = stages.send(values, lambda v, step=step: crossed(v, "wt", step))
            yield
            values = jnp.concatenate([values, got], axis=0)
            step //= 2
        yield stages.tie(values)

    def scattering(product):
        rows, step, total = span_rows, 1, None
        while step < wt_count:
            half_rows = rows // 2
            if total is None:
                got = stages.send(
                    product(half_rows, rows).astype(bf16), lambda v, step=step: crossed(v, "wt", step)
                )
                kept = stages.mark(product(0, half_rows))
            else:
                got = stages.send(
                    total[half_rows:].astype(bf16), lambda v, step=step: crossed(v, "wt", step)
                )
                kept = total[:half_rows]
            yield
            total = kept + stages.tie(got).astype(f32)
            rows, step = half_rows, step * 2
        yield total

    def side(array, a):
        return array[:, a * grp_count * shard_width : (a + 1) * grp_count * shard_width]

    def block(array, b, axis):
        return lax.slice_in_dim(array, b * shard_width, (b + 1) * shard_width, axis=axis)

    def whole(held, axis):
        return jnp.concatenate([held[p] for p in places], axis=axis)

    class Reduction:
        def __init__(self, axis):
            self.axis, self.sums = axis, {}

        def part(self, a, b):
            return block(self.products[a], b, self.axis)

        def seq(self):
            for b in ring:
                got = [by_seq.send(self.part(a, b), -a) for a in others]
                self.sums[b] = sum([g.astype(f32) for g in got], self.part(0, b).astype(f32))
                yield

        def grp(self):
            self.total = self.sums[ring[0]]
            for b in ring[1:]:
                got = by_grp.send(self.total.astype(bf16), 1)
                yield
                self.total = self.sums[b] + got.astype(f32)

        def grp_first(self):
            self.totals = {a: self.part(a, ring[0]) for a in backwards}
            for b in ring[1:]:
                for a in backwards:
                    got = by_grp.send(self.totals[a].astype(bf16), 1).astype(f32)
                    self.totals[a] = self.part(a, b).astype(f32) + got
                    yield

        def seq_last(self):
            self.total = self.totals[0]
            for a in others:
                got = by_seq.send(self.totals[a].astype(bf16), -a)
                self.total = self.total + got.astype(f32)

    def products(left, right, axis):
        result = {}
        for a in backwards:
            pair = (side(left, a), right) if axis == 0 else (left, side(right, a))
            result[a] = stages.mark(
                matmul(stages.tie(pair[0]), pair[1], contract_rows).astype(bf16)
            )
        return result

    def hidden_part(array, h):
        return array[..., h * half : (h + 1) * half]

    in_held = {(0, 0): in_weight.reshape(shard_width, 3 * channels)}
    out_held = {(0, 0): out_weight}
    gate_held = [
        {(0, 0): hidden_part(gate_up, h).reshape(shard_width, 2 * half)} for h in range(2)
    ]
    down_held = [{(0, 0): down_weight[h * half : (h + 1) * half]} for h in range(2)]
    in_grp, out_grp = grp_steps(in_held), grp_steps(out_held)
    gate_grp = [grp_steps(held) for held in gate_held]
    down_grp = [grp_steps(held, [0, *others]) for held in down_held]
    in_seq, out_seq = seq_steps(in_held), seq_steps(out_held)
    gate_seq = [seq_steps(held) for held in gate_held]
    down_seq = [seq_steps(held, [0]) for held in down_held]

    go(in_grp)
    go(in_seq)

    order_row = order[0]
    slot_blocks = order_row.reshape(peers, local_rows)
    here_positions = lax.dynamic_index_in_dim(slot_blocks, block_index, 0, keepdims=False)
    targets = here_positions // local_rows
    slots = jnp.arange(local_rows, dtype=jnp.int32)
    earlier = slots[:, None] < slots[None, :]
    same = (targets[:, None] == targets[None, :]) & earlier
    send_place = targets * per_peer + jnp.sum(same.astype(jnp.int32), axis=0)
    send_matrix = (slots[:, None] == send_place[None, :]).astype(bf16)
    mine = slot_blocks // local_rows == block_index
    mine_rank = matmul(mine.astype(bf16), earlier.astype(bf16)).astype(jnp.int32)
    sources = jnp.arange(peers, dtype=jnp.int32)
    arrival = jnp.where(mine, sources[:, None] * per_peer + mine_rank, -1).reshape(-1)
    home_place = order_row - block_index * local_rows
    home_hot = (home_place[:, None] == slots[None, :]).astype(bf16)
    arrival_hot = (arrival[:, None] == slots[None, :]).astype(bf16)

    def exchange(rows):
        return lax.all_to_all(rows, ("seq", "wt"), split_axis=0, concat_axis=0, tiled=True)

    tokens_got = stages.send(select_rows(send_matrix, tokens[0], plain), exchange)
    home_matrix = stages.mark(matmul(stages.tie(home_hot), arrival_hot, contract_rows).astype(bf16))
    cot_sent = stages.mark(select_rows(send_matrix, stages.tie(cotangent[0]), plain))

    def home_of(got):
        return relative(select_rows(home_matrix, stages.tie(got), plain))

    def to_arrival(rows):
        return stages.send(select_rows(home_matrix, relative(rows), contract_rows), exchange)

    def arrived(got):
        return select_rows(send_matrix, got, contract_rows)

    go(in_grp)
    go(in_seq)
    token_rows = home_of(tokens_got).astype(f32)
    mixer_row = relative(mixer_gain[None])
    feed_row = relative(feed_gain[None])
    scale_mix = rms_scale(token_rows)
    normed = gathering((token_rows * scale_mix * mixer_row).astype(bf16))
    next(normed)
    rest(in_grp)
    go(in_seq)
    go(out_grp)
    go(in_seq)
    next(normed)
    go(out_grp)
    go(out_seq)
    normed_all = next(normed)
    span_rows = normed_all.shape[0]
    rest(out_grp)
    go(gate_grp[0])
    go(out_seq)
    go(gate_grp[1])

    full_in = whole(in_held, 0)
    projected = matmul(stages.tie(normed_all), full_in)
    in_gate, out_gate, values = (
        projected[:, k * channels : (k + 1) * channels] for k in range(3)
    )
    gated = stages.mark((in_gate * values).astype(bf16))

    rel = peer_order(wt_count)
    place_of = jnp.array([rel.index(j) for j in range(wt_count)] + [wt_count], dtype=jnp.int32)
    block_at = [wt_at ^ j for j in rel]

    def taken(array, at):
        return lax.dynamic_index_in_dim(array, at, 0, keepdims=False)

    def row_of(block):
        return place_of[wt_at ^ block]

    tails = gated.reshape(wt_count, local_rows, channels)[:, -2:]
    carried = stages.send(
        taken(tails, row_of(wt_count - 1)), lambda v: passed_along(v, "seq", 1)
    )
    rest(out_seq)
    tails = jnp.concatenate([tails, stages.tie(carried)[None]], axis=0)
    before = jnp.stack(
        [
            taken(tails, jnp.where(at == 0, wt_count, row_of(jnp.maximum(at - 1, 0))))
            for at in block_at
        ]
    )
    extended = jnp.concatenate(
        [before, gated.reshape(wt_count, local_rows, channels)], axis=1
    ).astype(f32)
    positions = (
        (seq_at * wt_count + jnp.stack(block_at))[:, None] * local_rows + slots[None, :]
    )[:, :, None]
    docs = lengths.shape[1]
    starts = [sum([lengths[0, i] for i in range(d)], jnp.int32(0)) for d in range(docs)]

    def mask(at, back):
        opening = jnp.zeros_like(at)
        for start in starts:
            opening = jnp.where(start <= at, jnp.maximum(opening, start), opening)
        return (at - back >= opening).astype(f32)

    mask_one, mask_two = mask(positions, 1), mask(positions, 2)
    taps = conv_taps.astype(f32)
    now, one_back, two_back = extended[:, 2:], extended[:, 1:-1], extended[:, :-2]
    mixed = (taps[2] * now + mask_one * taps[1] * one_back + mask_two * taps[0] * two_back).reshape(
        span_rows, channels
    )
    mixed_out = stages.mark((out_gate * mixed).astype(bf16))
    go(gate_grp[0])
    go(gate_seq[0])
    full_out = whole(out_held, 1)
    branch = scattering(lambda i, j: matmul(stages.tie(mixed_out)[i:j], full_out))
    next(branch)
    go(gate_seq[0])
    next(branch)
    go(gate_grp[1])
    go(gate_grp[0])
    go(gate_seq[0])
    hidden_state = token_rows + next(branch)
    scale_feed = rms_scale(hidden_state)
    feed = gathering((hidden_state * scale_feed * feed_row).astype(bf16))
    next(feed)
    go(down_seq[0])
    cot_got = stages.send(cot_sent, exchange)
    go(gate_grp[1])
    next(feed)
    feed_all = next(feed)
    go(gate_seq[0])
    go(down_seq[1])
    go(down_grp[0])
    cot_rows = home_of(cot_got)
    cot = gathering(cot_rows)
    next(cot)
    go(down_grp[0])
    go(gate_seq[1])
    go(down_grp[0])

    full_gate, gate_part, up_part, activated = ({} for _ in range(4))
    full_down, gates_grad = {}, {}

    def forward_half(h):
        full_gate[h] = whole(gate_held[h], 0)
        source = stages.tie(feed_all)
        gate_part[h] = matmul(source, full_gate[h][:, :half])
        up_part[h] = matmul(source, full_gate[h][:, half:])
        activated[h] = stages.mark(
            (gate_part[h] * jax.nn.sigmoid(gate_part[h]) * up_part[h]).astype(bf16)
        )

    def backward_half(h):
        full_down[h] = whole(down_held[h], 1)
        act_grad = matmul(stages.tie(cot_all), full_down[h], contract_cols)
        gate, sigmoid_gate = gate_part[h], jax.nn.sigmoid(gate_part[h])
        gates_grad[h] = stages.mark(
            jnp.concatenate(
                [
                    (act_grad * up_part[h] * sigmoid_gate * (1.0 + gate * (1.0 - sigmoid_gate))).astype(
                        bf16
                    ),
                    (act_grad * gate * sigmoid_gate).astype(bf16),
                ],
                axis=1,
            )
        )

    gating, down = [Reduction(0), Reduction(0)], [Reduction(1), Reduction(1)]
    gating_seq, gating_grp = [g.seq() for g in gating], [g.grp() for g in gating]
    down_first, down_then = down[0].grp_first(), down[1].grp()
    down_swap = down[1].seq()
    forward_half(0)
    go(down_grp[0])
    go(gate_seq[1])
    next(cot)
    cot_all = next(cot)
    down[0].products = products(activated[0], cot_all, 1)
    go(down_grp[0])
    rest(down_grp[0])
    go(gate_seq[1])
    go(down_grp[1])
    rest(gate_seq[1])
    go(down_grp[1])
    backward_half(0)
    gating[0].products = products(feed_all, gates_grad[0], 0)
    go(down_grp[1], 2)
    go(gating_seq[0])
    rest(down_grp[1])
    go(gating_seq[0])
    forward_half(1)
    go(down_first)
    down[1].products = products(activated[1], cot_all, 1)
    go(down_first)
    go(gating_seq[0])
    backward_half(1)
    go(down_first)
    rest(gating_seq[0])
    gating[1].products = products(feed_all, gates_grad[1], 0)
    go(down_first)

    feed_norm = scattering(
        lambda i, j: sum(
            matmul(stages.tie(gates_grad[h])[i:j], full_gate[h], contract_cols) for h in range(2)
        )
    )
    next(feed_norm)
    go(down_swap)
    rest(down_first)
    next(feed_norm)
    go(down_swap)
    go(gating_grp[0])
    go(down_swap)
    go(gating_grp[0])
    go(down_swap)
    feed_norm_grad = next(feed_norm)
    feed_hat = hidden_state * scale_feed
    feed_term = jnp.sum(feed_norm_grad * feed_hat, axis=0)
    feed_scaled = feed_norm_grad * feed_row
    hidden_grad = cot_rows.astype(f32) + scale_feed * (
        feed_scaled - feed_hat * jnp.mean(feed_scaled * feed_hat, axis=-1, keepdims=True)
    )
    branch_back = gathering(hidden_grad.astype(bf16))
    next(branch_back)
    feed_out = scattering(
        lambda i, j: sum(matmul(stages.tie(activated[h])[i:j], full_down[h]) for h in range(2))
    )
    next(feed_out)
    go(gating_seq[1])
    rest(gating_grp[0])
    next(branch_back)
    branch_grad = next(branch_back)
    go(gating_seq[1])
    go(down_then)

    mixed_out_grad = matmul(stages.tie(branch_grad), full_out, contract_cols)
    out_gate_grad = (mixed_out_grad * mixed).astype(bf16)
    mixed_grad = stages.mark((mixed_out_grad * out_gate).astype(bf16))
    heads = mixed_grad.reshape(wt_count, local_rows, channels)[:, :2]
    incoming = stages.send(taken(heads, row_of(0)), lambda v: passed_along(v, "seq", -1))
    out_sum, in_sum = Reduction(1), Reduction(0)
    out_swap, out_ring = out_sum.seq(), out_sum.grp()
    in_swap, in_ring = in_sum.seq(), in_sum.grp()
    out_sum.products = products(mixed_out, branch_grad, 1)
    next(feed_out)
    go(gating_seq[1])
    go(down_then)
    rest(gating_seq[1], down_then)
    go(gating_grp[1])
    heads = jnp.concatenate([heads, stages.tie(incoming)[None]], axis=0)
    last = wt_count - 1
    behind = jnp.stack(
        [
            taken(heads, jnp.where(at == last, wt_count, row_of(jnp.minimum(at + 1, last))))
            for at in block_at
        ]
    )
    grad_ext = jnp.concatenate(
        [mixed_grad.reshape(wt_count, local_rows, channels), behind], axis=1
    ).astype(f32)
    mixed_low = grad_ext[:, :-2]
    gated_grad = (
        taps[2] * mixed_low
        + taps[1] * mask(positions + 1, 1) * grad_ext[:, 1:-1]
        + taps[0] * mask(positions + 2, 2) * grad_ext[:, 2:]
    )
    taps_term = jnp.stack(
        [
            jnp.sum(mixed_low * mask_two * two_back, axis=(0, 1)),
            jnp.sum(mixed_low * mask_one * one_back, axis=(0, 1)),
            jnp.sum(mixed_low * now, axis=(0, 1)),
        ]
    )
    gated_low = gated_grad.astype(bf16).astype(f32).reshape(span_rows, channels)
    projected_grad = stages.mark(
        jnp.concatenate(
            [(gated_low * values).astype(bf16), out_gate_grad, (gated_low * in_gate).astype(bf16)],
            axis=1,
        )
    )
    mix_norm = scattering(
        lambda i, j: matmul(stages.tie(projected_grad)[i:j], full_in, contract_cols)
    )
    next(mix_norm)
    go(out_swap)
    next(mix_norm)
    in_sum.products = products(normed_all, projected_grad, 0)
    go(gating_grp[1])
    go(out_swap)
    block_got = to_arrival((hidden_state + next(feed_out)).astype(bf16))
    rest(out_swap)
    rest(gating_grp[1])
    mix_norm_grad = next(mix_norm)
    mix_hat = token_rows * scale_mix
    mixer_term = jnp.sum(mix_norm_grad * mix_hat, axis=0)
    mix_scaled = mix_norm_grad * mixer_row
    grad_home = hidden_grad + scale_mix * (
        mix_scaled - mix_hat * jnp.mean(mix_scaled * mix_hat, axis=-1, keepdims=True)
    )
    grad_got = to_arrival(grad_home.astype(bf16))
    down[0].seq_last()
    go(in_swap, 2)
    rest(out_ring)
    go(in_swap)
    block_out = arrived(block_got)
    gains = summed(relative(jnp.stack([mixer_term, feed_term])), ("wt", "seq", "grp"))
    taps_grad = summed(taps_term, ("seq", "grp"))
    go(in_ring)
    rest(in_swap)
    tokens_grad = arrived(grad_got).astype(f32)
    rest(in_ring)
    out_grad = out_sum.total
    in_grad = in_sum.total.reshape(shard_width, 3, channels)
    down_grad = jnp.concatenate([d.total for d in down], axis=0)
    gating_grad = jnp.concatenate(
        [g.total.reshape(shard_width, 2, half) for g in gating], axis=2
    )
    return (
        block_out[None],
        tokens_grad[None],
        gains[0],
        gains[1],
        in_grad,
        taps_grad,
        out_grad,
        gating_grad,
        down_grad,
    )


def solution(mesh):
    in_specs = (
        P("grp", ("seq", "wt"), None),
        P("grp", None),
        P("grp", None),
        P(),
        P(),
        P(("seq", "grp"), None, "wt"),
        P(None, "wt"),
        P("wt", ("seq", "grp")),
        P(("seq", "grp"), None, "wt"),
        P("wt", ("seq", "grp")),
        P("grp", ("seq", "wt"), None),
    )
    out_specs = (
        P("grp", ("seq", "wt"), None),
        P("grp", ("seq", "wt"), None),
        P(),
        P(),
        P(("seq", "grp"), None, "wt"),
        P(None, "wt"),
        P("wt", ("seq", "grp")),
        P(("seq", "grp"), None, "wt"),
        P("wt", ("seq", "grp")),
    )
    return jax.shard_map(shards, mesh=mesh, in_specs=in_specs, out_specs=out_specs, check_vma=False)
```

```python
import jax
import jax.numpy as jnp
from jax import lax
from jax.sharding import PartitionSpec as P

epsilon = 1e-05
bf16 = jnp.bfloat16
f32 = jnp.float32
plain = (((1,), (0,)), ((), ()))
contract_rows = (((0,), (0,)), ((), ()))
contract_cols = (((1,), (1,)), ((), ()))


def rotated(array, axis, by):
    count = lax.axis_size(axis)
    return lax.ppermute(array, axis, [(i, (i + by) % count) for i in range(count)])


def crossed(array, axis, by):
    count = lax.axis_size(axis)
    return lax.ppermute(array, axis, [(i, i ^ by) for i in range(count)])


def passed_along(array, axis, by):
    count = lax.axis_size(axis)
    pairs = [(i, i + by) for i in range(count) if 0 <= i + by < count]
    return lax.ppermute(array, axis, pairs)


def after(array, *others):
    return lax.optimization_barrier((array, *others))[0]


class Sequence:
    def __init__(self):
        self.last = ()

    def tie(self, array, *others):
        return after(array, *self.last, *others) if self.last or others else array

    def mark(self, array):
        self.last = (array,)
        return array

    def got(self, array):
        return self.mark(self.tie(array))

    def send(self, array, move, *others):
        return move(self.mark(self.tie(array, *others)))


class Chain:
    def __init__(self, stages, axis, depth):
        self.stages, self.axis, self.depth = stages, axis, depth
        self.arrived = []

    def send(self, array, by):
        behind = self.arrived[-self.depth : len(self.arrived) - self.depth + 1]
        result = self.stages.send(array, lambda v: rotated(v, self.axis, by), *behind)
        self.arrived.append(result)
        return result

    def settle(self, back=1):
        self.stages.got(self.arrived[-back])


def go(steps, count=1):
    for _ in range(count):
        next(steps, None)


def rest(*all_steps):
    for steps in all_steps:
        for _ in steps:
            pass


def rms_scale(values):
    return lax.rsqrt(jnp.mean(values * values, axis=-1, keepdims=True) + epsilon)


def relative_columns(array, seq_at, grp_at, seq_count, grp_count):
    width = array.shape[1] // (seq_count * grp_count)
    blocks = {
        (a, b): array[:, (a * grp_count + b) * width : (a * grp_count + b + 1) * width]
        for a in range(seq_count)
        for b in range(grp_count)
    }
    blocks = {(a, b): blocks[(-a % seq_count, -b % grp_count)] for a, b in blocks}
    step = 1
    while step < seq_count:
        chosen = (seq_at // step) % 2 == 1
        blocks = {
            (a, b): jnp.where(chosen, blocks[((a - step) % seq_count, b)], blocks[(a, b)])
            for a, b in blocks
        }
        step *= 2
    step = 1
    while step < grp_count:
        chosen = (grp_at // step) % 2 == 1
        blocks = {
            (a, b): jnp.where(chosen, blocks[(a, (b - step) % grp_count)], blocks[(a, b)])
            for a, b in blocks
        }
        step *= 2
    return jnp.concatenate(
        [blocks[(a, b)] for a in range(seq_count) for b in range(grp_count)], axis=1
    )


def peer_order(count):
    order, step = [0], count // 2
    while step:
        order = order + [j ^ step for j in order]
        step //= 2
    return order


def summed(array, axes):
    for axis in axes:
        step = 1
        while step < lax.axis_size(axis):
            array = array + crossed(array, axis, step)
            step *= 2
    return array


def select_rows(matrix, rows, dims):
    return lax.dot_general(matrix, rows, dims, preferred_element_type=f32).astype(bf16)


def matmul(left, right, dims=plain):
    return lax.dot_general(left, right, dims, preferred_element_type=f32)


def shards(
    tokens,
    lengths,
    order,
    mixer_gain,
    feed_gain,
    in_weight,
    conv_taps,
    out_weight,
    gate_up,
    down_weight,
    cotangent,
):
    local_rows = tokens.shape[1]
    seq_count, wt_count, grp_count = (lax.axis_size(a) for a in ("seq", "wt", "grp"))
    seq_at, wt_at, grp_at = (lax.axis_index(a) for a in ("seq", "wt", "grp"))
    peers = seq_count * wt_count
    per_peer = local_rows // peers
    block_index = seq_at * wt_count + wt_at
    places = [(a, b) for a in range(seq_count) for b in range(grp_count)]
    others = range(1, seq_count)
    steps = range(1, grp_count)
    ring = list(steps) + [0]
    shard_width = in_weight.shape[0]
    channels = out_weight.shape[0]
    half = gate_up.shape[2] // 2
    def relative(array):
        return relative_columns(array, seq_at, grp_at, seq_count, grp_count)
    stages = Sequence()
    by_seq, by_grp = Chain(stages, "seq", 2), Chain(stages, "grp", 2)
    backwards = [*others, 0]
    def grp_steps(held, sides=(0,)):
        for b in steps:
            for a in sides:
                held[(a, b)] = by_grp.send(held[(a, b - 1)], 1)
                yield
    def seq_steps(held, at=None):
        for b in [0, *steps] if at is None else at:
            for a in others:
                held[(a, b)] = by_seq.send(held[(0, b)], a)
            yield
    def gathering(values):
        step = wt_count // 2
        while step:
            got = stages.send(values, lambda v, step=step: crossed(v, "wt", step))
            yield
            values = jnp.concatenate([values, got], axis=0)
            step //= 2
        yield stages.tie(values)
    def scattering(sent, kept):
        step = 1
        while step < wt_count:
            got = stages.send(sent.astype(bf16), lambda v, step=step: crossed(v, "wt", step))
            yield
            total = kept + stages.tie(got).astype(f32)
            kept, sent = (total[: total.shape[0] // 2], total[total.shape[0] // 2 :])
            step *= 2
        yield total
    def halves(array, axis=0):
        return jnp.split(array, 2, axis=axis)

    def into_width(grads):
        return jnp.einsum("ktc,kdc->td", grads, full_in, preferred_element_type=f32)
    def side(array, a):
        return array[:, a * grp_count * shard_width : (a + 1) * grp_count * shard_width]
    def block(array, b, axis):
        return lax.slice_in_dim(array, b * shard_width, (b + 1) * shard_width, axis=axis)
    def whole(held, axis):
        return jnp.concatenate([held[p] for p in places], axis=axis)
    class Reduction:
        def __init__(self, axis):
            self.axis, self.came = axis, {}

        def part(self, a, b):
            return block(self.products[a], b, self.axis)

        def seq(self):
            for b in ring:
                for a in others:
                    self.came[(a, b)] = by_seq.send(self.part(a, b), -a)
                yield

        def summed(self, b):
            return sum(
                [self.came[(a, b)].astype(f32) for a in others], self.part(0, b).astype(f32)
            )

        def grp(self):
            self.total = self.summed(ring[0])
            for b in ring[1:]:
                got = by_grp.send(self.total.astype(bf16), 1)
                yield
                self.total = self.summed(b) + got.astype(f32)

        def grp_first(self):
            self.totals = {a: self.part(a, ring[0]) for a in backwards}
            for b in ring[1:]:
                for a in backwards:
                    got = by_grp.send(self.totals[a].astype(bf16), 1).astype(f32)
                    self.totals[a] = self.part(a, b).astype(f32) + got
                    yield

        def seq_last(self):
            self.total = self.totals[0]
            for a in others:
                got = by_seq.send(self.totals[a].astype(bf16), -a)
                self.total = self.total + got.astype(f32)
    def producing(reduction, left, right):
        reduction.products = {}
        for a in backwards:
            if right.ndim == 3:
                product = jnp.einsum(
                    "td,ktc->kdc", stages.tie(side(left, a)), right, preferred_element_type=f32
                )
            elif reduction.axis == 0:
                product = matmul(stages.tie(side(left, a)), right, contract_rows)
            else:
                product = matmul(stages.tie(left), side(right, a), contract_rows)
            reduction.products[a] = stages.mark(product.astype(bf16))
            if a in (backwards[-2], backwards[-1]):
                yield
    def hidden_part(array, h):
        return array[..., h * half : (h + 1) * half]
    in_held = {(0, 0): in_weight.transpose(1, 0, 2)}
    out_held = {(0, 0): out_weight}
    gate_held = [
        {(0, 0): hidden_part(gate_up, h).reshape(shard_width, 2 * half)} for h in range(2)
    ]
    down_held = [{(0, 0): down_weight[h * half : (h + 1) * half]} for h in range(2)]
    in_grp, out_grp = grp_steps(in_held), grp_steps(out_held)
    gate_grp = [grp_steps(held) for held in gate_held]
    down_grp = [grp_steps(held, [0, *others]) for held in down_held]
    in_seq, out_seq = seq_steps(in_held), seq_steps(out_held)
    gate_seq = [seq_steps(held) for held in gate_held]
    down_seq = [seq_steps(held, [0]) for held in down_held]
    go(in_grp)
    go(in_seq)
    order_row = order[0]
    slot_blocks = order_row.reshape(peers, local_rows)
    here_positions = lax.dynamic_index_in_dim(slot_blocks, block_index, 0, keepdims=False)
    targets = here_positions // local_rows
    slots = jnp.arange(local_rows, dtype=jnp.int32)
    earlier = slots[:, None] < slots[None, :]
    same = (targets[:, None] == targets[None, :]) & earlier
    send_place = targets * per_peer + jnp.sum(same.astype(jnp.int32), axis=0)
    send_matrix = (slots[:, None] == send_place[None, :]).astype(bf16)
    mine = slot_blocks // local_rows == block_index
    mine_rank = matmul(mine.astype(bf16), earlier.astype(bf16)).astype(jnp.int32)
    sources = jnp.arange(peers, dtype=jnp.int32)
    arrival = jnp.where(mine, sources[:, None] * per_peer + mine_rank, -1).reshape(-1)
    home_place = order_row - block_index * local_rows
    home_hot = (home_place[:, None] == slots[None, :]).astype(bf16)
    arrival_hot = (arrival[:, None] == slots[None, :]).astype(bf16)
    def exchange(rows):
        return lax.all_to_all(rows, ("seq", "wt"), split_axis=0, concat_axis=0, tiled=True)
    tokens_got = stages.send(select_rows(send_matrix, tokens[0], plain), exchange)
    home_matrix = stages.mark(matmul(stages.tie(home_hot), arrival_hot, contract_rows).astype(bf16))
    by_grp.depth = 2
    by_seq.depth = 2
    cot_sent = stages.mark(select_rows(send_matrix, stages.tie(cotangent[0]), plain))
    def home_of(got):
        return relative(select_rows(home_matrix, stages.tie(got), plain))
    def to_arrival(rows):
        return stages.send(select_rows(home_matrix, relative(rows), contract_rows), exchange)
    def arrived(got):
        return select_rows(send_matrix, got, contract_rows)
    mixer_row = relative(mixer_gain[None])
    feed_row = relative(feed_gain[None])
    token_rows = home_of(tokens_got).astype(f32)
    scale_mix = rms_scale(token_rows)
    go(in_grp)
    go(in_seq)
    go(in_seq)
    normed = gathering((token_rows * scale_mix * mixer_row).astype(bf16))
    next(normed)
    go(in_grp)
    go(out_seq)
    by_grp.depth = 2
    go(out_grp)
    go(in_seq)
    go(out_grp)
    next(normed)
    normed_all = next(normed)
    span_rows = normed_all.shape[0]
    go(out_grp)
    full_in = whole(in_held, 1)
    go(gate_grp[1])
    go(out_seq)
    go(gate_grp[0])
    in_source = stages.tie(normed_all)
    go(out_seq)
    in_gate, out_gate, values = (matmul(in_source, full_in[k]) for k in range(3))
    gated = stages.mark((in_gate * values).astype(bf16))
    rel = peer_order(wt_count)
    place_of = jnp.array([rel.index(j) for j in range(wt_count)] + [wt_count], dtype=jnp.int32)
    block_at = [wt_at ^ j for j in rel]
    def taken(array, at):
        return lax.dynamic_index_in_dim(array, at, 0, keepdims=False)
    def row_of(block):
        return place_of[wt_at ^ block]
    tails = gated.reshape(wt_count, local_rows, channels)[:, -2:]
    carried = stages.send(
        taken(tails, row_of(wt_count - 1)), lambda v: passed_along(v, "seq", 1)
    )
    by_grp.depth = 3
    tails = jnp.concatenate([tails, stages.tie(carried)[None]], axis=0)
    go(out_seq)
    before = jnp.stack(
        [
            taken(tails, jnp.where(at == 0, wt_count, row_of(jnp.maximum(at - 1, 0))))
            for at in block_at
        ]
    )
    extended = jnp.concatenate(
        [before, gated.reshape(wt_count, local_rows, channels)], axis=1
    ).astype(f32)
    positions = (
        (seq_at * wt_count + jnp.stack(block_at))[:, None] * local_rows + slots[None, :]
    )[:, :, None]
    docs = lengths.shape[1]
    starts = [sum([lengths[0, i] for i in range(d)], jnp.int32(0)) for d in range(docs)]
    def mask(at, back):
        opening = jnp.zeros_like(at)
        for start in starts:
            opening = jnp.where(start <= at, jnp.maximum(opening, start), opening)
        return (at - back >= opening).astype(f32)
    mask_one, mask_two = mask(positions, 1), mask(positions, 2)
    taps = conv_taps.astype(f32)
    now, one_back, two_back = extended[:, 2:], extended[:, 1:-1], extended[:, :-2]
    mixed = (taps[2] * now + mask_one * taps[1] * one_back + mask_two * taps[0] * two_back).reshape(
        span_rows, channels
    )
    go(gate_seq[0])
    mixed_out = stages.mark((out_gate * mixed).astype(bf16))
    full_out = whole(out_held, 1)
    by_grp.settle()
    kept, sent = halves(stages.tie(mixed_out))
    kept = stages.mark(matmul(kept, full_out))
    sent = stages.mark(matmul(sent, full_out).astype(bf16))
    go(gate_grp[0])
    branch = scattering(sent, kept)
    next(branch)
    next(branch)
    go(gate_seq[0])
    go(down_seq[0])
    go(gate_grp[1])
    go(gate_seq[0])
    go(gate_grp[0])
    hidden_state = token_rows + next(branch)
    scale_feed = rms_scale(hidden_state)
    feed = gathering((hidden_state * scale_feed * feed_row).astype(bf16))
    next(feed)
    by_seq.settle()
    cot_got = stages.send(cot_sent, exchange)
    go(gate_grp[1])
    go(gate_seq[0])
    next(feed)
    feed_all = next(feed)
    go(down_grp[0])
    go(down_seq[1])
    cot_rows = home_of(cot_got)
    cot = gathering(cot_rows)
    next(cot)
    by_grp.depth = 3
    go(down_grp[0])
    go(gate_seq[1])
    go(down_grp[0])
    full_gate, gate_part, up_part, activated = ({} for _ in range(4))
    full_down, gates_grad = {}, {}
    def forward_half(h):
        full_gate[h] = whole(gate_held[h], 0)
        source = stages.tie(feed_all)
        gate_part[h] = matmul(source, full_gate[h][:, :half])
        up_part[h] = matmul(source, full_gate[h][:, half:])
        activated[h] = stages.mark(
            (gate_part[h] * jax.nn.sigmoid(gate_part[h]) * up_part[h]).astype(bf16)
        )
    forward_half(0)
    def backward_half(h):
        full_down[h] = whole(down_held[h], 1)
        act_grad = matmul(stages.tie(cot_all), full_down[h], contract_cols)
        gate, sigmoid_gate = gate_part[h], jax.nn.sigmoid(gate_part[h])
        gates_grad[h] = stages.mark(
            jnp.concatenate(
                [
                    (act_grad * up_part[h] * sigmoid_gate * (1.0 + gate * (1.0 - sigmoid_gate))).astype(
                        bf16
                    ),
                    (act_grad * gate * sigmoid_gate).astype(bf16),
                ],
                axis=1,
            )
        )
    gating, down = [Reduction(0), Reduction(0)], [Reduction(1), Reduction(1)]
    gating_seq, gating_grp = [g.seq() for g in gating], [g.grp() for g in gating]
    down_first, down_then = down[0].grp_first(), down[1].grp()
    down_swap = down[1].seq()
    go(down_grp[0])
    go(down_grp[0])
    go(gate_seq[1])
    next(cot)
    go(down_grp[0])
    cot_all = next(cot)
    go(gate_seq[1])
    rest(producing(down[0], activated[0], cot_all))
    go(gate_seq[1])
    go(down_grp[1])
    by_seq.settle(2)
    go(down_grp[1])
    rest(down_grp[0])
    backward_half(0)
    by_seq.settle(2)
    gating_work = producing(gating[0], feed_all, gates_grad[0])
    go(gating_work)
    go(down_grp[1])
    go(gating_seq[0])
    go(gating_work)
    go(down_grp[1])
    go(down_grp[1])
    by_grp.depth = 3
    rest(gate_seq[1])
    go(gating_seq[0])
    go(down_grp[1])
    go(gating_seq[0])
    forward_half(1)
    go(down_first)
    go(down_first)
    rest(producing(down[1], activated[1], cot_all))
    go(down_first)
    rest(down_grp[1])
    backward_half(1)
    go(down_first)
    gating_work = producing(gating[1], feed_all, gates_grad[1])
    go(down_swap)
    go(gating_work)
    go(gating_seq[0])
    by_grp.depth = 3
    go(down_first)
    norm_grad = stages.mark(
        matmul(stages.tie(gates_grad[0]), full_gate[0], contract_cols)
    )
    go(down_swap)
    go(gating_work)
    norm_grad = stages.mark(
        norm_grad + matmul(stages.tie(gates_grad[1]), full_gate[1], contract_cols)
    )
    kept, sent = halves(norm_grad)
    go(down_swap)
    feed_norm = scattering(sent, kept)
    next(feed_norm)
    next(feed_norm)
    go(down_swap)
    go(down_first)
    go(gating_grp[0])
    go(gating_seq[1])
    go(gating_seq[1])
    by_grp.depth = 1
    feed_norm_grad = next(feed_norm)
    feed_hat = hidden_state * scale_feed
    feed_term = jnp.sum(feed_norm_grad * feed_hat, axis=0)
    feed_scaled = feed_norm_grad * feed_row
    hidden_grad = cot_rows.astype(f32) + scale_feed * (
        feed_scaled - feed_hat * jnp.mean(feed_scaled * feed_hat, axis=-1, keepdims=True)
    )
    go(gating_grp[0])
    branch_back = gathering(hidden_grad.astype(bf16))
    by_grp.depth = 2
    next(branch_back)
    by_seq.settle(2)
    fed = stages.mark(matmul(stages.tie(activated[0]), full_down[0]))
    go(gating_grp[0])
    rest(gating_grp[0])
    fed = stages.mark(fed + matmul(stages.tie(activated[1]), full_down[1]))
    by_grp.settle()
    go(down_then)
    next(branch_back)
    branch_grad = next(branch_back)
    kept, sent = halves(fed)
    feed_out = scattering(sent, kept)
    mixed_out_grad = matmul(stages.tie(branch_grad), full_out, contract_cols)
    next(feed_out)
    out_gate_grad = (mixed_out_grad * mixed).astype(bf16)
    mixed_grad = stages.mark((mixed_out_grad * out_gate).astype(bf16))
    heads = mixed_grad.reshape(wt_count, local_rows, channels)[:, :2]
    incoming = stages.send(taken(heads, row_of(0)), lambda v: passed_along(v, "seq", -1))
    by_seq.settle()
    by_seq.settle()
    by_seq.settle(2)
    out_sum, in_sum = Reduction(1), Reduction(1)
    out_swap, out_ring = out_sum.seq(), out_sum.grp()
    in_swap, in_ring = in_sum.seq(), in_sum.grp()
    by_grp.depth = 2
    rest(producing(out_sum, mixed_out, branch_grad))
    next(feed_out)
    go(gating_seq[1])
    go(down_then)
    go(down_then)
    go(gating_seq[1])
    rest(down_then)
    by_seq.settle()
    go(gating_grp[1])
    heads = jnp.concatenate([heads, stages.tie(incoming)[None]], axis=0)
    by_grp.depth = 2
    last = wt_count - 1
    behind = jnp.stack(
        [
            taken(heads, jnp.where(at == last, wt_count, row_of(jnp.minimum(at + 1, last))))
            for at in block_at
        ]
    )
    grad_ext = jnp.concatenate(
        [mixed_grad.reshape(wt_count, local_rows, channels), behind], axis=1
    ).astype(f32)
    mixed_low = grad_ext[:, :-2]
    gated_grad = (
        taps[2] * mixed_low
        + taps[1] * mask(positions + 1, 1) * grad_ext[:, 1:-1]
        + taps[0] * mask(positions + 2, 2) * grad_ext[:, 2:]
    )
    taps_term = jnp.stack(
        [
            jnp.sum(mixed_low * mask_two * two_back, axis=(0, 1)),
            jnp.sum(mixed_low * mask_one * one_back, axis=(0, 1)),
            jnp.sum(mixed_low * now, axis=(0, 1)),
        ]
    )
    gated_low = gated_grad.astype(bf16).astype(f32).reshape(span_rows, channels)
    projected_grad = stages.mark(
        jnp.stack(
            [(gated_low * values).astype(bf16), out_gate_grad, (gated_low * in_gate).astype(bf16)]
        )
    )
    in_work = producing(in_sum, normed_all, projected_grad)
    by_grp.depth = 2
    kept, sent = halves(stages.tie(projected_grad), 1)
    go(out_swap)
    sent = stages.mark(into_width(sent).astype(bf16))
    kept = stages.mark(into_width(kept))
    by_grp.depth = 1
    mix_norm = scattering(sent, kept)
    next(mix_norm)
    go(gating_grp[1])
    go(in_work)
    next(mix_norm)
    go(in_work)
    go(out_swap)
    go(out_swap)
    go(out_swap)
    go(gating_grp[1])
    block_got = to_arrival((hidden_state + next(feed_out)).astype(bf16))
    rest(gating_grp[1])
    mix_norm_grad = next(mix_norm)
    mix_hat = token_rows * scale_mix
    mixer_term = jnp.sum(mix_norm_grad * mix_hat, axis=0)
    mix_scaled = mix_norm_grad * mixer_row
    grad_home = hidden_grad + scale_mix * (
        mix_scaled - mix_hat * jnp.mean(mix_scaled * mix_hat, axis=-1, keepdims=True)
    )
    grad_got = to_arrival(grad_home.astype(bf16))
    down[0].seq_last()
    by_seq.settle()
    go(in_swap)
    go(out_ring)
    go(in_swap)
    go(out_ring)
    go(out_ring)
    rest(out_ring)
    block_out = arrived(block_got)
    gains = summed(relative(jnp.stack([mixer_term, feed_term])), ("wt", "seq", "grp"))
    taps_grad = summed(taps_term, ("seq", "grp"))
    go(in_swap)
    go(in_ring)
    tokens_grad = arrived(grad_got).astype(f32)
    go(in_ring)
    go(in_swap)
    go(in_ring)
    rest(in_ring)
    out_grad = out_sum.total
    in_grad = in_sum.total.transpose(1, 0, 2)
    down_grad = jnp.concatenate([d.total for d in down], axis=0)
    gating_grad = jnp.concatenate(
        [g.total.reshape(shard_width, 2, half) for g in gating], axis=2
    )
    return (
        block_out[None],
        tokens_grad[None],
        gains[0],
        gains[1],
        in_grad,
        taps_grad,
        out_grad,
        gating_grad,
        down_grad,
    )


def solution(mesh):
    in_specs = (
        P("grp", ("seq", "wt"), None),
        P("grp", None),
        P("grp", None),
        P(),
        P(),
        P(("seq", "grp"), None, "wt"),
        P(None, "wt"),
        P("wt", ("seq", "grp")),
        P(("seq", "grp"), None, "wt"),
        P("wt", ("seq", "grp")),
        P("grp", ("seq", "wt"), None),
    )
    out_specs = (
        P("grp", ("seq", "wt"), None),
        P("grp", ("seq", "wt"), None),
        P(),
        P(),
        P(("seq", "grp"), None, "wt"),
        P(None, "wt"),
        P("wt", ("seq", "grp")),
        P(("seq", "grp"), None, "wt"),
        P("wt", ("seq", "grp")),
    )
    return jax.shard_map(shards, mesh=mesh, in_specs=in_specs, out_specs=out_specs, check_vma=False)
```

```python
import jax
import jax.numpy as jnp
from jax import lax
from jax.sharding import PartitionSpec as P

epsilon = 1e-05
bf16 = jnp.bfloat16
f32 = jnp.float32
plain = (((1,), (0,)), ((), ()))
contract_rows = (((0,), (0,)), ((), ()))
contract_cols = (((1,), (1,)), ((), ()))


def rotated(array, axis, by):
    count = lax.axis_size(axis)
    return lax.ppermute(array, axis, [(i, (i + by) % count) for i in range(count)])


def crossed(array, axis, by):
    count = lax.axis_size(axis)
    return lax.ppermute(array, axis, [(i, i ^ by) for i in range(count)])


def passed_along(array, axis, by):
    count = lax.axis_size(axis)
    pairs = [(i, i + by) for i in range(count) if 0 <= i + by < count]
    return lax.ppermute(array, axis, pairs)


def after(array, *others):
    return lax.optimization_barrier((array, *others))[0]


class Sequence:
    def __init__(self):
        self.last = ()

    def tie(self, array, *others):
        return after(array, *self.last, *others) if self.last or others else array

    def mark(self, array):
        self.last = (array,)
        return array

    def got(self, array):
        return self.mark(self.tie(array))

    def send(self, array, move, *others):
        return move(self.mark(self.tie(array, *others)))


class Chain:
    def __init__(self, stages, axis, depth):
        self.stages, self.axis, self.depth = stages, axis, depth
        self.arrived = []

    def send(self, array, by):
        behind = self.arrived[-self.depth : len(self.arrived) - self.depth + 1]
        result = self.stages.send(array, lambda v: rotated(v, self.axis, by), *behind)
        self.arrived.append(result)
        return result

    def settle(self, back=1):
        self.stages.got(self.arrived[-back])


def go(steps, count=1):
    for _ in range(count):
        next(steps, None)


def rest(*all_steps):
    for steps in all_steps:
        for _ in steps:
            pass


def rms_scale(values):
    return lax.rsqrt(jnp.mean(values * values, axis=-1, keepdims=True) + epsilon)


def relative_columns(array, seq_at, grp_at, seq_count, grp_count):
    width = array.shape[1] // (seq_count * grp_count)
    blocks = {
        (a, b): array[:, (a * grp_count + b) * width : (a * grp_count + b + 1) * width]
        for a in range(seq_count)
        for b in range(grp_count)
    }
    blocks = {(a, b): blocks[(-a % seq_count, -b % grp_count)] for a, b in blocks}
    step = 1
    while step < seq_count:
        chosen = (seq_at // step) % 2 == 1
        blocks = {
            (a, b): jnp.where(chosen, blocks[((a - step) % seq_count, b)], blocks[(a, b)])
            for a, b in blocks
        }
        step *= 2
    step = 1
    while step < grp_count:
        chosen = (grp_at // step) % 2 == 1
        blocks = {
            (a, b): jnp.where(chosen, blocks[(a, (b - step) % grp_count)], blocks[(a, b)])
            for a, b in blocks
        }
        step *= 2
    return jnp.concatenate(
        [blocks[(a, b)] for a in range(seq_count) for b in range(grp_count)], axis=1
    )


def peer_order(count):
    order, step = [0], count // 2
    while step:
        order = order + [j ^ step for j in order]
        step //= 2
    return order


def summed(array, axes):
    for axis in axes:
        step = 1
        while step < lax.axis_size(axis):
            array = array + crossed(array, axis, step)
            step *= 2
    return array


def select_rows(matrix, rows, dims):
    return lax.dot_general(matrix, rows, dims, preferred_element_type=f32).astype(bf16)


def matmul(left, right, dims=plain):
    return lax.dot_general(left, right, dims, preferred_element_type=f32)


def shards(
    tokens,
    lengths,
    order,
    mixer_gain,
    feed_gain,
    in_weight,
    conv_taps,
    out_weight,
    gate_up,
    down_weight,
    cotangent,
):
    local_rows = tokens.shape[1]
    seq_count, wt_count, grp_count = (lax.axis_size(a) for a in ("seq", "wt", "grp"))
    seq_at, wt_at, grp_at = (lax.axis_index(a) for a in ("seq", "wt", "grp"))
    peers = seq_count * wt_count
    per_peer = local_rows // peers
    block_index = seq_at * wt_count + wt_at
    places = [(a, b) for a in range(seq_count) for b in range(grp_count)]
    others = range(1, seq_count)
    steps = range(1, grp_count)
    ring = list(steps) + [0]
    shard_width = in_weight.shape[0]
    channels = out_weight.shape[0]
    half = gate_up.shape[2] // 2
    def relative(array):
        return relative_columns(array, seq_at, grp_at, seq_count, grp_count)
    stages = Sequence()
    by_seq, by_grp = Chain(stages, "seq", 2), Chain(stages, "grp", 2)
    backwards = [*others, 0]
    def grp_steps(held, sides=(0,)):
        for b in steps:
            for a in sides:
                held[(a, b)] = by_grp.send(held[(a, b - 1)], 1)
                yield
    def side_steps(held):
        moving = None
        for b in steps:
            if moving is None:
                moving = jnp.concatenate([held[(a, 0)] for a in range(seq_count)], axis=1)
            moving = by_grp.send(moving, 1)
            for a in range(seq_count):
                held[(a, b)] = block(moving, a, 1)
            yield
    def seq_steps(held, at=None):
        for b in [0, *steps] if at is None else at:
            for a in others:
                held[(a, b)] = by_seq.send(held[(0, b)], a)
            yield
    def gathering(values):
        step = wt_count // 2
        while step:
            got = stages.send(values, lambda v, step=step: crossed(v, "wt", step))
            yield
            values = jnp.concatenate([values, got], axis=0)
            step //= 2
        yield stages.tie(values)
    def scattering(sent, kept):
        step = 1
        while step < wt_count:
            got = stages.send(sent.astype(bf16), lambda v, step=step: crossed(v, "wt", step))
            yield
            total = kept + stages.tie(got).astype(f32)
            kept, sent = (total[: total.shape[0] // 2], total[total.shape[0] // 2 :])
            step *= 2
        yield total
    def halves(array, axis=0):
        return jnp.split(array, 2, axis=axis)
    def into_width(grads):
        return jnp.einsum("ktc,kdc->td", grads, full_in, preferred_element_type=f32)
    def side(array, a):
        return array[:, a * grp_count * shard_width : (a + 1) * grp_count * shard_width]
    def block(array, b, axis):
        return lax.slice_in_dim(array, b * shard_width, (b + 1) * shard_width, axis=axis)
    def whole(held, axis):
        return jnp.concatenate([held[p] for p in places], axis=axis)
    class Reduction:
        def __init__(self, axis):
            self.axis, self.came = axis, {}

        def part(self, a, b):
            return block(self.products[a], b, self.axis)

        def seq(self, size=1):
            for group in [ring[i : i + size] for i in range(0, grp_count, size)]:
                for a in others:
                    sent = [self.part(a, b) for b in group]
                    got = by_seq.send(
                        sent[0] if len(sent) == 1 else jnp.concatenate(sent, axis=self.axis), -a
                    )
                    for i, b in enumerate(group):
                        self.came[(a, b)] = block(got, i, self.axis)
                yield

        def summed(self, b):
            return sum(
                [self.came[(a, b)].astype(f32) for a in others], self.part(0, b).astype(f32)
            )

        def grp(self):
            self.total = self.summed(ring[0])
            for b in ring[1:]:
                got = by_grp.send(self.total.astype(bf16), 1)
                yield
                self.total = self.summed(b) + got.astype(f32)

        def grp_first(self):
            def both(b):
                return jnp.concatenate([self.part(a, b) for a in [0, *others]], axis=self.axis)

            self.totals = both(ring[0])
            for b in ring[1:]:
                got = by_grp.send(self.totals.astype(bf16), 1)
                yield
                self.totals = both(b).astype(f32) + got.astype(f32)

        def seq_last(self):
            self.total = block(self.totals, 0, self.axis)
            for a in others:
                got = by_seq.send(block(self.totals, a, self.axis).astype(bf16), -a)
                self.total = self.total + got.astype(f32)
    def producing(reduction, left, right):
        reduction.products = {}
        for a in backwards:
            if right.ndim == 3:
                product = jnp.einsum(
                    "td,ktc->kdc", stages.tie(side(left, a)), right, preferred_element_type=f32
                )
            elif reduction.axis == 0:
                product = matmul(stages.tie(side(left, a)), right, contract_rows)
            else:
                product = matmul(stages.tie(left), side(right, a), contract_rows)
            reduction.products[a] = stages.mark(product.astype(bf16))
            if a in (backwards[-2], backwards[-1]):
                yield
    def hidden_part(array, h):
        return array[..., h * half : (h + 1) * half]
    in_held = {(0, 0): in_weight.transpose(1, 0, 2)}
    out_held = {(0, 0): out_weight}
    gate_held = [
        {(0, 0): hidden_part(gate_up, h).reshape(shard_width, 2 * half)} for h in range(2)
    ]
    down_held = [{(0, 0): down_weight[h * half : (h + 1) * half]} for h in range(2)]
    in_grp, out_grp = grp_steps(in_held), grp_steps(out_held)
    gate_grp = [grp_steps(held) for held in gate_held]
    down_grp = [side_steps(held) for held in down_held]
    in_seq, out_seq = seq_steps(in_held), seq_steps(out_held)
    gate_seq = [seq_steps(held) for held in gate_held]
    down_seq = [seq_steps(held, [0]) for held in down_held]
    go(in_seq)
    go(in_grp)
    order_row = order[0]
    slot_blocks = order_row.reshape(peers, local_rows)
    here_positions = lax.dynamic_index_in_dim(slot_blocks, block_index, 0, keepdims=False)
    targets = here_positions // local_rows
    slots = jnp.arange(local_rows, dtype=jnp.int32)
    earlier = slots[:, None] < slots[None, :]
    same = (targets[:, None] == targets[None, :]) & earlier
    send_place = targets * per_peer + jnp.sum(same.astype(jnp.int32), axis=0)
    send_matrix = (slots[:, None] == send_place[None, :]).astype(bf16)
    mine = slot_blocks // local_rows == block_index
    mine_rank = matmul(mine.astype(bf16), earlier.astype(bf16)).astype(jnp.int32)
    sources = jnp.arange(peers, dtype=jnp.int32)
    arrival = jnp.where(mine, sources[:, None] * per_peer + mine_rank, -1).reshape(-1)
    home_place = order_row - block_index * local_rows
    home_hot = (home_place[:, None] == slots[None, :]).astype(bf16)
    arrival_hot = (arrival[:, None] == slots[None, :]).astype(bf16)
    def exchange(rows):
        return lax.all_to_all(rows, ("seq", "wt"), split_axis=0, concat_axis=0, tiled=True)
    by_grp.depth = 2
    tokens_got = stages.send(select_rows(send_matrix, tokens[0], plain), exchange)
    home_matrix = stages.mark(matmul(stages.tie(home_hot), arrival_hot, contract_rows).astype(bf16))
    by_seq.depth = 2
    cot_sent = stages.mark(select_rows(send_matrix, stages.tie(cotangent[0]), plain))
    def home_of(got):
        return relative(select_rows(home_matrix, stages.tie(got), plain))
    def to_arrival(rows):
        return stages.send(select_rows(home_matrix, relative(rows), contract_rows), exchange)
    def arrived(got):
        return select_rows(send_matrix, got, contract_rows)
    mixer_row = relative(mixer_gain[None])
    feed_row = relative(feed_gain[None])
    go(in_grp)
    token_rows = home_of(tokens_got).astype(f32)
    scale_mix = rms_scale(token_rows)
    go(in_seq)
    go(in_seq)
    normed = gathering((token_rows * scale_mix * mixer_row).astype(bf16))
    next(normed)
    go(in_grp)
    go(out_seq)
    by_grp.depth = 2
    go(out_grp)
    go(out_grp)
    go(in_seq)
    next(normed)
    normed_all = next(normed)
    span_rows = normed_all.shape[0]
    go(out_seq)
    go(out_grp)
    full_in = whole(in_held, 1)
    go(gate_grp[0])
    go(gate_grp[1])
    in_source = stages.tie(normed_all)
    in_gate, out_gate, values = (matmul(in_source, full_in[k]) for k in range(3))
    gated = stages.mark((in_gate * values).astype(bf16))
    go(out_seq)
    rel = peer_order(wt_count)
    place_of = jnp.array([rel.index(j) for j in range(wt_count)] + [wt_count], dtype=jnp.int32)
    block_at = [wt_at ^ j for j in rel]
    def taken(array, at):
        return lax.dynamic_index_in_dim(array, at, 0, keepdims=False)
    def row_of(block):
        return place_of[wt_at ^ block]
    tails = gated.reshape(wt_count, local_rows, channels)[:, -2:]
    carried = stages.send(
        taken(tails, row_of(wt_count - 1)), lambda v: passed_along(v, "seq", 1)
    )
    by_grp.depth = 3
    tails = jnp.concatenate([tails, stages.tie(carried)[None]], axis=0)
    go(out_seq)
    before = jnp.stack(
        [
            taken(tails, jnp.where(at == 0, wt_count, row_of(jnp.maximum(at - 1, 0))))
            for at in block_at
        ]
    )
    extended = jnp.concatenate(
        [before, gated.reshape(wt_count, local_rows, channels)], axis=1
    ).astype(f32)
    positions = (
        (seq_at * wt_count + jnp.stack(block_at))[:, None] * local_rows + slots[None, :]
    )[:, :, None]
    docs = lengths.shape[1]
    starts = [sum([lengths[0, i] for i in range(d)], jnp.int32(0)) for d in range(docs)]
    def mask(at, back):
        opening = jnp.zeros_like(at)
        for start in starts:
            opening = jnp.where(start <= at, jnp.maximum(opening, start), opening)
        return (at - back >= opening).astype(f32)
    mask_one, mask_two = mask(positions, 1), mask(positions, 2)
    taps = conv_taps.astype(f32)
    now, one_back, two_back = extended[:, 2:], extended[:, 1:-1], extended[:, :-2]
    mixed = (taps[2] * now + mask_one * taps[1] * one_back + mask_two * taps[0] * two_back).reshape(
        span_rows, channels
    )
    go(gate_seq[0])
    by_grp.settle()
    mixed_out = stages.mark((out_gate * mixed).astype(bf16))
    full_out = whole(out_held, 1)
    kept, sent = halves(stages.tie(mixed_out))
    kept = stages.mark(matmul(kept, full_out))
    sent = stages.mark(matmul(sent, full_out).astype(bf16))
    branch = scattering(sent, kept)
    go(gate_grp[0])
    go(gate_seq[0])
    next(branch)
    next(branch)
    go(down_seq[0])
    go(gate_grp[1])
    hidden_state = token_rows + next(branch)
    go(gate_seq[0])
    scale_feed = rms_scale(hidden_state)
    go(down_seq[1])
    feed = gathering((hidden_state * scale_feed * feed_row).astype(bf16))
    go(gate_grp[0])
    by_seq.settle()
    next(feed)
    cot_got = stages.send(cot_sent, exchange)
    go(gate_grp[1])
    go(gate_seq[0])
    next(feed)
    feed_all = next(feed)
    go(down_grp[0])
    cot_rows = home_of(cot_got)
    cot = gathering(cot_rows)
    by_grp.settle(2)
    go(gate_seq[1])
    next(cot)
    by_grp.depth = 3
    full_gate, gate_part, up_part, activated = ({} for _ in range(4))
    full_down, gates_grad = {}, {}
    def forward_half(h):
        full_gate[h] = whole(gate_held[h], 0)
        source = stages.tie(feed_all)
        gate_part[h] = matmul(source, full_gate[h][:, :half])
        up_part[h] = matmul(source, full_gate[h][:, half:])
        activated[h] = stages.mark(
            (gate_part[h] * jax.nn.sigmoid(gate_part[h]) * up_part[h]).astype(bf16)
        )
    forward_half(0)
    go(gate_seq[1])
    def backward_half(h):
        full_down[h] = whole(down_held[h], 1)
        act_grad = matmul(stages.tie(cot_all), full_down[h], contract_cols)
        gate, sigmoid_gate = gate_part[h], jax.nn.sigmoid(gate_part[h])
        gates_grad[h] = stages.mark(
            jnp.concatenate(
                [
                    (act_grad * up_part[h] * sigmoid_gate * (1.0 + gate * (1.0 - sigmoid_gate))).astype(
                        bf16
                    ),
                    (act_grad * gate * sigmoid_gate).astype(bf16),
                ],
                axis=1,
            )
        )
    gating, down = [Reduction(0), Reduction(0)], [Reduction(1), Reduction(1)]
    gating_seq, gating_grp = [g.seq() for g in gating], [g.grp() for g in gating]
    down_first, down_then = down[0].grp_first(), down[1].grp()
    down_swap = down[1].seq(2)
    go(down_grp[0])
    next(cot)
    go(down_grp[0])
    go(gate_seq[1])
    cot_all = next(cot)
    by_grp.settle(2)
    rest(producing(down[0], activated[0], cot_all))
    go(gate_seq[1])
    by_seq.settle(2)
    go(down_grp[1])
    go(down_grp[1])
    rest(down_grp[0])
    backward_half(0)
    by_seq.settle(2)
    gating_work = producing(gating[0], feed_all, gates_grad[0])
    go(gating_work)
    go(down_grp[1])
    go(gating_seq[0])
    go(gating_seq[0])
    by_grp.depth = 3
    rest(gate_seq[1])
    go(down_first)
    go(gating_seq[0])
    by_grp.depth = 1
    forward_half(1)
    go(down_first)
    go(gating_work)
    rest(producing(down[1], activated[1], cot_all))
    go(down_swap)
    rest(down_grp[1])
    backward_half(1)
    go(down_first)
    go(down_swap)
    go(down_first)
    go(down_first)
    go(gating_seq[0])
    gating_work = producing(gating[1], feed_all, gates_grad[1])
    go(gating_work)
    by_seq.settle()
    norm_grad = stages.mark(
        matmul(stages.tie(gates_grad[0]), full_gate[0], contract_cols)
    )
    by_grp.depth = 3
    go(gating_work)
    norm_grad = stages.mark(
        norm_grad + matmul(stages.tie(gates_grad[1]), full_gate[1], contract_cols)
    )
    go(down_swap)
    kept, sent = halves(norm_grad)
    feed_norm = scattering(sent, kept)
    next(feed_norm)
    next(feed_norm)
    go(down_swap)
    go(gating_seq[1])
    by_grp.settle(2)
    by_grp.settle(2)
    by_grp.settle()
    go(down_first)
    go(gating_grp[0])
    by_grp.depth = 1
    feed_norm_grad = next(feed_norm)
    go(gating_seq[1])
    feed_hat = hidden_state * scale_feed
    feed_term = jnp.sum(feed_norm_grad * feed_hat, axis=0)
    feed_scaled = feed_norm_grad * feed_row
    hidden_grad = cot_rows.astype(f32) + scale_feed * (
        feed_scaled - feed_hat * jnp.mean(feed_scaled * feed_hat, axis=-1, keepdims=True)
    )
    go(gating_grp[0])
    by_grp.depth = 3
    branch_back = gathering(hidden_grad.astype(bf16))
    by_grp.depth = 2
    next(branch_back)
    by_seq.settle(2)
    fed = stages.mark(matmul(stages.tie(activated[0]), full_down[0]))
    go(gating_grp[0])
    rest(gating_grp[0])
    fed = stages.mark(fed + matmul(stages.tie(activated[1]), full_down[1]))
    by_grp.settle()
    go(down_then)
    next(branch_back)
    branch_grad = next(branch_back)
    mixed_out_grad = matmul(stages.tie(branch_grad), full_out, contract_cols)
    kept, sent = halves(fed)
    feed_out = scattering(sent, kept)
    by_seq.settle()
    next(feed_out)
    out_gate_grad = (mixed_out_grad * mixed).astype(bf16)
    mixed_grad = stages.mark((mixed_out_grad * out_gate).astype(bf16))
    heads = mixed_grad.reshape(wt_count, local_rows, channels)[:, :2]
    by_seq.settle()
    by_seq.settle(2)
    incoming = stages.send(taken(heads, row_of(0)), lambda v: passed_along(v, "seq", -1))
    out_sum, in_sum = Reduction(1), Reduction(1)
    out_swap, out_ring = out_sum.seq(), out_sum.grp()
    in_swap, in_ring = in_sum.seq(), in_sum.grp()
    by_grp.depth = 2
    rest(producing(out_sum, mixed_out, branch_grad))
    next(feed_out)
    go(down_then)
    go(gating_seq[1])
    go(down_then)
    go(gating_seq[1])
    rest(down_then)
    by_seq.settle()
    go(gating_grp[1])
    heads = jnp.concatenate([heads, stages.tie(incoming)[None]], axis=0)
    by_grp.depth = 2
    last = wt_count - 1
    behind = jnp.stack(
        [
            taken(heads, jnp.where(at == last, wt_count, row_of(jnp.minimum(at + 1, last))))
            for at in block_at
        ]
    )
    grad_ext = jnp.concatenate(
        [mixed_grad.reshape(wt_count, local_rows, channels), behind], axis=1
    ).astype(f32)
    mixed_low = grad_ext[:, :-2]
    gated_grad = (
        taps[2] * mixed_low
        + taps[1] * mask(positions + 1, 1) * grad_ext[:, 1:-1]
        + taps[0] * mask(positions + 2, 2) * grad_ext[:, 2:]
    )
    taps_term = jnp.stack(
        [
            jnp.sum(mixed_low * mask_two * two_back, axis=(0, 1)),
            jnp.sum(mixed_low * mask_one * one_back, axis=(0, 1)),
            jnp.sum(mixed_low * now, axis=(0, 1)),
        ]
    )
    gated_low = gated_grad.astype(bf16).astype(f32).reshape(span_rows, channels)
    projected_grad = stages.mark(
        jnp.stack(
            [(gated_low * values).astype(bf16), out_gate_grad, (gated_low * in_gate).astype(bf16)]
        )
    )
    in_work = producing(in_sum, normed_all, projected_grad)
    kept, sent = halves(stages.tie(projected_grad), 1)
    by_seq.settle()
    by_grp.depth = 2
    go(out_swap)
    sent = stages.mark(into_width(sent).astype(bf16))
    kept = stages.mark(into_width(kept))
    by_grp.depth = 1
    by_grp.settle()
    mix_norm = scattering(sent, kept)
    next(mix_norm)
    go(gating_grp[1])
    go(in_work)
    next(mix_norm)
    go(out_swap)
    go(in_work)
    go(out_swap)
    go(out_swap)
    go(gating_grp[1])
    mix_norm_grad = next(mix_norm)
    by_grp.settle(2)
    block_got = to_arrival((hidden_state + next(feed_out)).astype(bf16))
    rest(gating_grp[1])
    mix_hat = token_rows * scale_mix
    mixer_term = jnp.sum(mix_norm_grad * mix_hat, axis=0)
    mix_scaled = mix_norm_grad * mixer_row
    grad_home = hidden_grad + scale_mix * (
        mix_scaled - mix_hat * jnp.mean(mix_scaled * mix_hat, axis=-1, keepdims=True)
    )
    grad_got = to_arrival(grad_home.astype(bf16))
    down[0].seq_last()
    by_seq.settle()
    go(in_swap)
    go(out_ring)
    go(out_ring)
    by_seq.settle()
    go(in_swap)
    go(out_ring)
    rest(out_ring)
    block_out = arrived(block_got)
    gains = summed(relative(jnp.stack([mixer_term, feed_term])), ("wt", "seq", "grp"))
    taps_grad = summed(taps_term, ("seq", "grp"))
    tokens_grad = arrived(grad_got).astype(f32)
    go(in_ring)
    go(in_ring)
    go(in_swap)
    go(in_swap)
    by_grp.settle()
    go(in_ring)
    rest(in_ring)
    out_grad = out_sum.total
    in_grad = in_sum.total.transpose(1, 0, 2)
    down_grad = jnp.concatenate([d.total for d in down], axis=0)
    gating_grad = jnp.concatenate(
        [g.total.reshape(shard_width, 2, half) for g in gating], axis=2
    )
    return (
        block_out[None],
        tokens_grad[None],
        gains[0],
        gains[1],
        in_grad,
        taps_grad,
        out_grad,
        gating_grad,
        down_grad,
    )


def solution(mesh):
    in_specs = (
        P("grp", ("seq", "wt"), None),
        P("grp", None),
        P("grp", None),
        P(),
        P(),
        P(("seq", "grp"), None, "wt"),
        P(None, "wt"),
        P("wt", ("seq", "grp")),
        P(("seq", "grp"), None, "wt"),
        P("wt", ("seq", "grp")),
        P("grp", ("seq", "wt"), None),
    )
    out_specs = (
        P("grp", ("seq", "wt"), None),
        P("grp", ("seq", "wt"), None),
        P(),
        P(),
        P(("seq", "grp"), None, "wt"),
        P(None, "wt"),
        P("wt", ("seq", "grp")),
        P(("seq", "grp"), None, "wt"),
        P("wt", ("seq", "grp")),
    )
    return jax.shard_map(shards, mesh=mesh, in_specs=in_specs, out_specs=out_specs, check_vma=False)
```

```python
import jax
import jax.numpy as jnp
from jax import lax
from jax.sharding import PartitionSpec as P

epsilon = 1e-05
bf16 = jnp.bfloat16
f32 = jnp.float32
plain = (((1,), (0,)), ((), ()))
contract_rows = (((0,), (0,)), ((), ()))
contract_cols = (((1,), (1,)), ((), ()))


def rotated(array, axis, by):
    count = lax.axis_size(axis)
    return lax.ppermute(array, axis, [(i, (i + by) % count) for i in range(count)])


def crossed(array, axis, by):
    count = lax.axis_size(axis)
    return lax.ppermute(array, axis, [(i, i ^ by) for i in range(count)])


def passed_along(array, axis, by):
    count = lax.axis_size(axis)
    pairs = [(i, i + by) for i in range(count) if 0 <= i + by < count]
    return lax.ppermute(array, axis, pairs)


def after(array, *others):
    return lax.optimization_barrier((array, *others))[0]


class Sequence:
    def __init__(self):
        self.last = ()

    def tie(self, array, *others):
        return after(array, *self.last, *others) if self.last or others else array

    def mark(self, array):
        self.last = (array,)
        return array

    def got(self, array):
        return self.mark(self.tie(array))

    def send(self, array, move, *others):
        return move(self.mark(self.tie(array, *others)))


class Chain:
    def __init__(self, stages, axis, depth):
        self.stages, self.axis, self.depth = stages, axis, depth
        self.arrived = []

    def send(self, array, by):
        behind = self.arrived[-self.depth : len(self.arrived) - self.depth + 1]
        result = self.stages.send(array, lambda v: rotated(v, self.axis, by), *behind)
        self.arrived.append(result)
        return result

    def settle(self, back=1):
        self.stages.got(self.arrived[-back])


def go(steps, count=1):
    for _ in range(count):
        next(steps, None)


def rest(*all_steps):
    for steps in all_steps:
        for _ in steps:
            pass


def rms_scale(values):
    return lax.rsqrt(jnp.mean(values * values, axis=-1, keepdims=True) + epsilon)


def relative_columns(array, seq_at, grp_at, seq_count, grp_count):
    width = array.shape[1] // (seq_count * grp_count)
    blocks = {
        (a, b): array[:, (a * grp_count + b) * width : (a * grp_count + b + 1) * width]
        for a in range(seq_count)
        for b in range(grp_count)
    }
    blocks = {(a, b): blocks[(-a % seq_count, -b % grp_count)] for a, b in blocks}
    step = 1
    while step < seq_count:
        chosen = (seq_at // step) % 2 == 1
        blocks = {
            (a, b): jnp.where(chosen, blocks[((a - step) % seq_count, b)], blocks[(a, b)])
            for a, b in blocks
        }
        step *= 2
    step = 1
    while step < grp_count:
        chosen = (grp_at // step) % 2 == 1
        blocks = {
            (a, b): jnp.where(chosen, blocks[(a, (b - step) % grp_count)], blocks[(a, b)])
            for a, b in blocks
        }
        step *= 2
    return jnp.concatenate(
        [blocks[(a, b)] for a in range(seq_count) for b in range(grp_count)], axis=1
    )


def peer_order(count):
    order, step = [0], count // 2
    while step:
        order = order + [j ^ step for j in order]
        step //= 2
    return order


def summed(array, axes):
    for axis in axes:
        step = 1
        while step < lax.axis_size(axis):
            array = array + crossed(array, axis, step)
            step *= 2
    return array


def select_rows(matrix, rows, dims):
    return lax.dot_general(matrix, rows, dims, preferred_element_type=f32).astype(bf16)


def matmul(left, right, dims=plain):
    return lax.dot_general(left, right, dims, preferred_element_type=f32)


def shards(
    tokens,
    lengths,
    order,
    mixer_gain,
    feed_gain,
    in_weight,
    conv_taps,
    out_weight,
    gate_up,
    down_weight,
    cotangent,
):
    local_rows = tokens.shape[1]
    seq_count, wt_count, grp_count = (lax.axis_size(a) for a in ("seq", "wt", "grp"))
    seq_at, wt_at, grp_at = (lax.axis_index(a) for a in ("seq", "wt", "grp"))
    peers = seq_count * wt_count
    per_peer = local_rows // peers
    block_index = seq_at * wt_count + wt_at
    places = [(a, b) for a in range(seq_count) for b in range(grp_count)]
    others = range(1, seq_count)
    steps = range(1, grp_count)
    ring = list(steps) + [0]
    shard_width = in_weight.shape[0]
    channels = out_weight.shape[0]
    half = gate_up.shape[2] // 2
    def relative(array):
        return relative_columns(array, seq_at, grp_at, seq_count, grp_count)
    stages = Sequence()
    by_seq, by_grp = Chain(stages, "seq", 2), Chain(stages, "grp", 2)
    backwards = [*others, 0]
    def grp_steps(held, sides=(0,)):
        for b in steps:
            for a in sides:
                held[(a, b)] = by_grp.send(held[(a, b - 1)], 1)
                yield
    def side_steps(held):
        moving = None
        for b in steps:
            if moving is None:
                moving = jnp.concatenate([held[(a, 0)] for a in range(seq_count)], axis=1)
            moving = by_grp.send(moving, 1)
            for a in range(seq_count):
                held[(a, b)] = block(moving, a, 1)
            yield
    def seq_steps(held, at=None):
        for b in [0, *steps] if at is None else at:
            for a in others:
                held[(a, b)] = by_seq.send(held[(0, b)], a)
            yield
    def gathering(values):
        step = wt_count // 2
        while step:
            got = stages.send(values, lambda v, step=step: crossed(v, "wt", step))
            yield
            values = jnp.concatenate([values, got], axis=0)
            step //= 2
        yield stages.tie(values)
    def scattering(sent, kept):
        step = 1
        while step < wt_count:
            got = stages.send(sent.astype(bf16), lambda v, step=step: crossed(v, "wt", step))
            yield
            total = kept + stages.tie(got).astype(f32)
            kept, sent = (total[: total.shape[0] // 2], total[total.shape[0] // 2 :])
            step *= 2
        yield total
    def halves(array, axis=0):
        return jnp.split(array, 2, axis=axis)
    def into_width(grads):
        return jnp.einsum("ktc,kdc->td", grads, full_in, preferred_element_type=f32)
    def side(array, a):
        return array[:, a * grp_count * shard_width : (a + 1) * grp_count * shard_width]
    def block(array, b, axis):
        return lax.slice_in_dim(array, b * shard_width, (b + 1) * shard_width, axis=axis)
    def whole(held, axis):
        return jnp.concatenate([held[p] for p in places], axis=axis)
    class Reduction:
        def __init__(self, axis):
            self.axis, self.came = axis, {}

        def part(self, a, b):
            return block(self.products[a], b, self.axis)

        def seq(self, size=1):
            for group in [ring[i : i + size] for i in range(0, grp_count, size)]:
                for a in others:
                    sent = [self.part(a, b) for b in group]
                    got = by_seq.send(
                        sent[0] if len(sent) == 1 else jnp.concatenate(sent, axis=self.axis), -a
                    )
                    for i, b in enumerate(group):
                        self.came[(a, b)] = block(got, i, self.axis)
                yield

        def summed(self, b):
            return sum(
                [self.came[(a, b)].astype(f32) for a in others], self.part(0, b).astype(f32)
            )

        def grp(self):
            self.total = self.summed(ring[0])
            for b in ring[1:]:
                got = by_grp.send(self.total.astype(bf16), 1)
                yield
                self.total = self.summed(b) + got.astype(f32)

        def grp_first(self):
            def both(b):
                return jnp.concatenate([self.part(a, b) for a in [0, *others]], axis=self.axis)

            self.totals = both(ring[0])
            for b in ring[1:]:
                got = by_grp.send(self.totals.astype(bf16), 1)
                yield
                self.totals = both(b).astype(f32) + got.astype(f32)

        def seq_last(self):
            self.total = block(self.totals, 0, self.axis)
            for a in others:
                got = by_seq.send(block(self.totals, a, self.axis).astype(bf16), -a)
                self.total = self.total + got.astype(f32)
    def producing(reduction, left, right):
        reduction.products = {}
        for a in backwards:
            if right.ndim == 3:
                product = jnp.einsum(
                    "td,ktc->kdc", stages.tie(side(left, a)), right, preferred_element_type=f32
                )
            elif reduction.axis == 0:
                product = matmul(stages.tie(side(left, a)), right, contract_rows)
            else:
                product = matmul(stages.tie(left), side(right, a), contract_rows)
            reduction.products[a] = stages.mark(product.astype(bf16))
            if a in (backwards[-2], backwards[-1]):
                yield
    def hidden_part(array, h):
        return array[..., h * half : (h + 1) * half]
    in_held = {(0, 0): in_weight.transpose(1, 0, 2)}
    out_held = {(0, 0): out_weight}
    gate_held = [
        {(0, 0): hidden_part(gate_up, h).reshape(shard_width, 2 * half)} for h in range(2)
    ]
    down_held = [{(0, 0): down_weight[h * half : (h + 1) * half]} for h in range(2)]
    in_grp, out_grp = grp_steps(in_held), grp_steps(out_held)
    gate_grp = [grp_steps(held) for held in gate_held]
    down_grp = [side_steps(held) for held in down_held]
    in_seq, out_seq = seq_steps(in_held), seq_steps(out_held)
    gate_seq = [seq_steps(held) for held in gate_held]
    down_seq = [seq_steps(held, [0]) for held in down_held]
    go(in_seq)
    go(in_grp)
    order_row = order[0]
    slot_blocks = order_row.reshape(peers, local_rows)
    here_positions = lax.dynamic_index_in_dim(slot_blocks, block_index, 0, keepdims=False)
    targets = here_positions // local_rows
    slots = jnp.arange(local_rows, dtype=jnp.int32)
    earlier = slots[:, None] < slots[None, :]
    same = (targets[:, None] == targets[None, :]) & earlier
    send_place = targets * per_peer + jnp.sum(same.astype(jnp.int32), axis=0)
    send_matrix = (slots[:, None] == send_place[None, :]).astype(bf16)
    mine = slot_blocks // local_rows == block_index
    mine_rank = matmul(mine.astype(bf16), earlier.astype(bf16)).astype(jnp.int32)
    sources = jnp.arange(peers, dtype=jnp.int32)
    arrival = jnp.where(mine, sources[:, None] * per_peer + mine_rank, -1).reshape(-1)
    home_place = order_row - block_index * local_rows
    home_hot = (home_place[:, None] == slots[None, :]).astype(bf16)
    arrival_hot = (arrival[:, None] == slots[None, :]).astype(bf16)
    def exchange(rows):
        return lax.all_to_all(rows, ("seq", "wt"), split_axis=0, concat_axis=0, tiled=True)
    by_grp.depth = 2
    tokens_got = stages.send(select_rows(send_matrix, tokens[0], plain), exchange)
    home_matrix = stages.mark(matmul(stages.tie(home_hot), arrival_hot, contract_rows).astype(bf16))
    by_seq.depth = 2
    cot_sent = stages.mark(select_rows(send_matrix, stages.tie(cotangent[0]), plain))
    def home_of(got):
        return relative(select_rows(home_matrix, stages.tie(got), plain))
    def to_arrival(rows):
        return stages.send(select_rows(home_matrix, relative(rows), contract_rows), exchange)
    def arrived(got):
        return select_rows(send_matrix, got, contract_rows)
    mixer_row = relative(mixer_gain[None])
    feed_row = relative(feed_gain[None])
    go(in_grp)
    token_rows = home_of(tokens_got).astype(f32)
    scale_mix = rms_scale(token_rows)
    go(in_seq)
    go(in_seq)
    normed = gathering((token_rows * scale_mix * mixer_row).astype(bf16))
    next(normed)
    go(in_grp)
    by_seq.depth = 2
    go(out_seq)
    go(out_grp)
    by_grp.depth = 2
    go(out_grp)
    go(in_seq)
    next(normed)
    normed_all = next(normed)
    span_rows = normed_all.shape[0]
    go(out_seq)
    go(out_grp)
    full_in = whole(in_held, 1)
    go(gate_grp[0])
    go(gate_grp[1])
    in_source = stages.tie(normed_all)
    in_gate, out_gate, values = (matmul(in_source, full_in[k]) for k in range(3))
    gated = stages.mark((in_gate * values).astype(bf16))
    go(out_seq)
    rel = peer_order(wt_count)
    place_of = jnp.array([rel.index(j) for j in range(wt_count)] + [wt_count], dtype=jnp.int32)
    block_at = [wt_at ^ j for j in rel]
    def taken(array, at):
        return lax.dynamic_index_in_dim(array, at, 0, keepdims=False)
    def row_of(block):
        return place_of[wt_at ^ block]
    tails = gated.reshape(wt_count, local_rows, channels)[:, -2:]
    carried = stages.send(
        taken(tails, row_of(wt_count - 1)), lambda v: passed_along(v, "seq", 1)
    )
    by_grp.depth = 3
    tails = jnp.concatenate([tails, stages.tie(carried)[None]], axis=0)
    go(out_seq)
    before = jnp.stack(
        [
            taken(tails, jnp.where(at == 0, wt_count, row_of(jnp.maximum(at - 1, 0))))
            for at in block_at
        ]
    )
    extended = jnp.concatenate(
        [before, gated.reshape(wt_count, local_rows, channels)], axis=1
    ).astype(f32)
    positions = (
        (seq_at * wt_count + jnp.stack(block_at))[:, None] * local_rows + slots[None, :]
    )[:, :, None]
    docs = lengths.shape[1]
    starts = [sum([lengths[0, i] for i in range(d)], jnp.int32(0)) for d in range(docs)]
    def mask(at, back):
        opening = jnp.zeros_like(at)
        for start in starts:
            opening = jnp.where(start <= at, jnp.maximum(opening, start), opening)
        return (at - back >= opening).astype(f32)
    mask_one, mask_two = mask(positions, 1), mask(positions, 2)
    taps = conv_taps.astype(f32)
    now, one_back, two_back = extended[:, 2:], extended[:, 1:-1], extended[:, :-2]
    mixed = (taps[2] * now + mask_one * taps[1] * one_back + mask_two * taps[0] * two_back).reshape(
        span_rows, channels
    )
    go(gate_seq[0])
    by_grp.settle()
    mixed_out = stages.mark((out_gate * mixed).astype(bf16))
    full_out = whole(out_held, 1)
    kept, sent = halves(stages.tie(mixed_out))
    kept = stages.mark(matmul(kept, full_out))
    sent = stages.mark(matmul(sent, full_out).astype(bf16))
    branch = scattering(sent, kept)
    go(gate_seq[0])
    go(gate_grp[0])
    next(branch)
    next(branch)
    go(down_seq[0])
    go(gate_grp[1])
    hidden_state = token_rows + next(branch)
    go(gate_seq[0])
    scale_feed = rms_scale(hidden_state)
    go(down_seq[1])
    feed = gathering((hidden_state * scale_feed * feed_row).astype(bf16))
    go(gate_grp[0])
    next(feed)
    by_seq.settle()
    go(gate_grp[1])
    cot_got = stages.send(cot_sent, exchange)
    go(gate_seq[0])
    go(gate_seq[1])
    next(feed)
    feed_all = next(feed)
    go(down_grp[0])
    cot_rows = home_of(cot_got)
    cot = gathering(cot_rows)
    go(gate_seq[1])
    by_grp.settle(2)
    next(cot)
    by_grp.depth = 3
    full_gate, gate_part, up_part, activated = ({} for _ in range(4))
    full_down, gates_grad = {}, {}
    def forward_half(h):
        full_gate[h] = whole(gate_held[h], 0)
        source = stages.tie(feed_all)
        gate_part[h] = matmul(source, full_gate[h][:, :half])
        up_part[h] = matmul(source, full_gate[h][:, half:])
        activated[h] = stages.mark(
            (gate_part[h] * jax.nn.sigmoid(gate_part[h]) * up_part[h]).astype(bf16)
        )
    forward_half(0)
    def backward_half(h):
        full_down[h] = whole(down_held[h], 1)
        act_grad = matmul(stages.tie(cot_all), full_down[h], contract_cols)
        gate, sigmoid_gate = gate_part[h], jax.nn.sigmoid(gate_part[h])
        gates_grad[h] = stages.mark(
            jnp.concatenate(
                [
                    (act_grad * up_part[h] * sigmoid_gate * (1.0 + gate * (1.0 - sigmoid_gate))).astype(
                        bf16
                    ),
                    (act_grad * gate * sigmoid_gate).astype(bf16),
                ],
                axis=1,
            )
        )
    gating, down = [Reduction(0), Reduction(0)], [Reduction(1), Reduction(1)]
    gating_seq, gating_grp = [g.seq() for g in gating], [g.grp() for g in gating]
    down_first, down_then = down[0].grp_first(), down[1].grp()
    down_swap = down[1].seq(2)
    go(down_grp[0])
    go(gate_seq[1])
    next(cot)
    go(down_grp[0])
    by_grp.settle(2)
    cot_all = next(cot)
    rest(producing(down[0], activated[0], cot_all))
    go(gate_seq[1])
    by_seq.settle(2)
    go(down_grp[1])
    go(down_grp[1])
    rest(down_grp[0])
    backward_half(0)
    gating_work = producing(gating[0], feed_all, gates_grad[0])
    by_seq.settle(2)
    by_grp.depth = 3
    go(gating_work)
    go(gating_seq[0])
    go(down_grp[1])
    go(gating_seq[0])
    rest(gate_seq[1])
    go(down_first)
    go(gating_seq[0])
    forward_half(1)
    by_grp.depth = 1
    rest(producing(down[1], activated[1], cot_all))
    go(gating_work)
    go(down_swap)
    go(down_first)
    rest(down_grp[1])
    backward_half(1)
    go(down_first)
    go(down_first)
    go(down_swap)
    go(down_first)
    go(gating_seq[0])
    gating_work = producing(gating[1], feed_all, gates_grad[1])
    go(gating_work)
    by_seq.settle()
    by_grp.depth = 3
    norm_grad = stages.mark(
        matmul(stages.tie(gates_grad[0]), full_gate[0], contract_cols)
    )
    go(gating_work)
    go(down_swap)
    norm_grad = stages.mark(
        norm_grad + matmul(stages.tie(gates_grad[1]), full_gate[1], contract_cols)
    )
    kept, sent = halves(norm_grad)
    feed_norm = scattering(sent, kept)
    next(feed_norm)
    next(feed_norm)
    go(down_swap)
    go(gating_seq[1])
    by_grp.settle(2)
    by_grp.settle(2)
    by_grp.settle()
    go(gating_grp[0])
    go(down_first)
    feed_norm_grad = next(feed_norm)
    go(gating_seq[1])
    by_grp.depth = 1
    feed_hat = hidden_state * scale_feed
    feed_term = jnp.sum(feed_norm_grad * feed_hat, axis=0)
    feed_scaled = feed_norm_grad * feed_row
    hidden_grad = cot_rows.astype(f32) + scale_feed * (
        feed_scaled - feed_hat * jnp.mean(feed_scaled * feed_hat, axis=-1, keepdims=True)
    )
    go(gating_grp[0])
    branch_back = gathering(hidden_grad.astype(bf16))
    by_grp.depth = 2
    next(branch_back)
    by_grp.depth = 3
    go(down_then)
    by_seq.settle(2)
    fed = stages.mark(matmul(stages.tie(activated[0]), full_down[0]))
    go(gating_grp[0])
    rest(gating_grp[0])
    fed = stages.mark(fed + matmul(stages.tie(activated[1]), full_down[1]))
    by_grp.settle()
    next(branch_back)
    branch_grad = next(branch_back)
    mixed_out_grad = matmul(stages.tie(branch_grad), full_out, contract_cols)
    kept, sent = halves(fed)
    feed_out = scattering(sent, kept)
    next(feed_out)
    out_gate_grad = (mixed_out_grad * mixed).astype(bf16)
    mixed_grad = stages.mark((mixed_out_grad * out_gate).astype(bf16))
    heads = mixed_grad.reshape(wt_count, local_rows, channels)[:, :2]
    by_seq.settle(2)
    by_seq.settle()
    incoming = stages.send(taken(heads, row_of(0)), lambda v: passed_along(v, "seq", -1))
    out_sum, in_sum = Reduction(1), Reduction(1)
    out_swap, out_ring = out_sum.seq(), out_sum.grp()
    in_swap, in_ring = in_sum.seq(), in_sum.grp()
    by_grp.depth = 2
    rest(producing(out_sum, mixed_out, branch_grad))
    next(feed_out)
    go(down_then)
    by_seq.depth = 2
    go(gating_seq[1])
    go(gating_seq[1])
    go(down_then)
    rest(down_then)
    by_seq.settle()
    by_grp.depth = 2
    go(gating_grp[1])
    heads = jnp.concatenate([heads, stages.tie(incoming)[None]], axis=0)
    last = wt_count - 1
    behind = jnp.stack(
        [
            taken(heads, jnp.where(at == last, wt_count, row_of(jnp.minimum(at + 1, last))))
            for at in block_at
        ]
    )
    grad_ext = jnp.concatenate(
        [mixed_grad.reshape(wt_count, local_rows, channels), behind], axis=1
    ).astype(f32)
    mixed_low = grad_ext[:, :-2]
    gated_grad = (
        taps[2] * mixed_low
        + taps[1] * mask(positions + 1, 1) * grad_ext[:, 1:-1]
        + taps[0] * mask(positions + 2, 2) * grad_ext[:, 2:]
    )
    taps_term = jnp.stack(
        [
            jnp.sum(mixed_low * mask_two * two_back, axis=(0, 1)),
            jnp.sum(mixed_low * mask_one * one_back, axis=(0, 1)),
            jnp.sum(mixed_low * now, axis=(0, 1)),
        ]
    )
    gated_low = gated_grad.astype(bf16).astype(f32).reshape(span_rows, channels)
    projected_grad = stages.mark(
        jnp.stack(
            [(gated_low * values).astype(bf16), out_gate_grad, (gated_low * in_gate).astype(bf16)]
        )
    )
    by_seq.settle(2)
    in_work = producing(in_sum, normed_all, projected_grad)
    kept, sent = halves(stages.tie(projected_grad), 1)
    by_seq.settle()
    go(out_swap)
    sent = stages.mark(into_width(sent).astype(bf16))
    kept = stages.mark(into_width(kept))
    by_grp.settle()
    by_grp.depth = 1
    mix_norm = scattering(sent, kept)
    next(mix_norm)
    go(gating_grp[1])
    go(in_work)
    next(mix_norm)
    go(out_swap)
    go(in_work)
    go(out_swap)
    go(out_swap)
    go(gating_grp[1])
    mix_norm_grad = next(mix_norm)
    by_grp.settle(2)
    block_got = to_arrival((hidden_state + next(feed_out)).astype(bf16))
    rest(gating_grp[1])
    mix_hat = token_rows * scale_mix
    mixer_term = jnp.sum(mix_norm_grad * mix_hat, axis=0)
    mix_scaled = mix_norm_grad * mixer_row
    grad_home = hidden_grad + scale_mix * (
        mix_scaled - mix_hat * jnp.mean(mix_scaled * mix_hat, axis=-1, keepdims=True)
    )
    grad_got = to_arrival(grad_home.astype(bf16))
    down[0].seq_last()
    by_seq.settle()
    go(in_swap)
    go(out_ring)
    go(out_ring)
    go(in_swap)
    go(out_ring)
    by_seq.settle()
    rest(out_ring)
    block_out = arrived(block_got)
    gains = summed(relative(jnp.stack([mixer_term, feed_term])), ("wt", "seq", "grp"))
    taps_grad = summed(taps_term, ("seq", "grp"))
    tokens_grad = arrived(grad_got).astype(f32)
    go(in_swap)
    go(in_ring)
    go(in_swap)
    by_grp.settle()
    go(in_ring)
    go(in_ring)
    rest(in_ring)
    out_grad = out_sum.total
    in_grad = in_sum.total.transpose(1, 0, 2)
    down_grad = jnp.concatenate([d.total for d in down], axis=0)
    gating_grad = jnp.concatenate(
        [g.total.reshape(shard_width, 2, half) for g in gating], axis=2
    )
    return (
        block_out[None],
        tokens_grad[None],
        gains[0],
        gains[1],
        in_grad,
        taps_grad,
        out_grad,
        gating_grad,
        down_grad,
    )


def solution(mesh):
    in_specs = (
        P("grp", ("seq", "wt"), None),
        P("grp", None),
        P("grp", None),
        P(),
        P(),
        P(("seq", "grp"), None, "wt"),
        P(None, "wt"),
        P("wt", ("seq", "grp")),
        P(("seq", "grp"), None, "wt"),
        P("wt", ("seq", "grp")),
        P("grp", ("seq", "wt"), None),
    )
    out_specs = (
        P("grp", ("seq", "wt"), None),
        P("grp", ("seq", "wt"), None),
        P(),
        P(),
        P(("seq", "grp"), None, "wt"),
        P(None, "wt"),
        P("wt", ("seq", "grp")),
        P(("seq", "grp"), None, "wt"),
        P("wt", ("seq", "grp")),
    )
    return jax.shard_map(shards, mesh=mesh, in_specs=in_specs, out_specs=out_specs, check_vma=False)
```

```python
import jax
import jax.numpy as jnp
from jax import lax
from jax.sharding import PartitionSpec as P

epsilon = 1e-05
bf16 = jnp.bfloat16
f32 = jnp.float32
plain = (((1,), (0,)), ((), ()))
contract_rows = (((0,), (0,)), ((), ()))
contract_cols = (((1,), (1,)), ((), ()))


def rotated(array, axis, by):
    count = lax.axis_size(axis)
    return lax.ppermute(array, axis, [(i, (i + by) % count) for i in range(count)])


def crossed(array, axis, by):
    count = lax.axis_size(axis)
    return lax.ppermute(array, axis, [(i, i ^ by) for i in range(count)])


def passed_along(array, axis, by):
    count = lax.axis_size(axis)
    pairs = [(i, i + by) for i in range(count) if 0 <= i + by < count]
    return lax.ppermute(array, axis, pairs)


def after(array, *others):
    return lax.optimization_barrier((array, *others))[0]


class Sequence:
    def __init__(self):
        self.last = ()

    def tie(self, array, *others):
        return after(array, *self.last, *others) if self.last or others else array

    def mark(self, array):
        self.last = (array,)
        return array

    def got(self, array):
        return self.mark(self.tie(array))

    def send(self, array, move, *others):
        return move(self.mark(self.tie(array, *others)))


class Chain:
    def __init__(self, stages, axis, depth):
        self.stages, self.axis, self.depth = stages, axis, depth
        self.arrived = []

    def send(self, array, by):
        behind = self.arrived[-self.depth : len(self.arrived) - self.depth + 1]
        result = self.stages.send(array, lambda v: rotated(v, self.axis, by), *behind)
        self.arrived.append(result)
        return result

    def settle(self, back=1):
        self.stages.got(self.arrived[-back])


def go(steps, count=1):
    for _ in range(count):
        next(steps, None)


def rest(*all_steps):
    for steps in all_steps:
        for _ in steps:
            pass


def rms_scale(values):
    return lax.rsqrt(jnp.mean(values * values, axis=-1, keepdims=True) + epsilon)


def relative_columns(array, seq_at, grp_at, seq_count, grp_count):
    width = array.shape[1] // (seq_count * grp_count)
    blocks = {
        (a, b): array[:, (a * grp_count + b) * width : (a * grp_count + b + 1) * width]
        for a in range(seq_count)
        for b in range(grp_count)
    }
    blocks = {(a, b): blocks[(-a % seq_count, -b % grp_count)] for a, b in blocks}
    step = 1
    while step < seq_count:
        chosen = (seq_at // step) % 2 == 1
        blocks = {
            (a, b): jnp.where(chosen, blocks[((a - step) % seq_count, b)], blocks[(a, b)])
            for a, b in blocks
        }
        step *= 2
    step = 1
    while step < grp_count:
        chosen = (grp_at // step) % 2 == 1
        blocks = {
            (a, b): jnp.where(chosen, blocks[(a, (b - step) % grp_count)], blocks[(a, b)])
            for a, b in blocks
        }
        step *= 2
    return jnp.concatenate(
        [blocks[(a, b)] for a in range(seq_count) for b in range(grp_count)], axis=1
    )


def peer_order(count):
    order, step = [0], count // 2
    while step:
        order = order + [j ^ step for j in order]
        step //= 2
    return order


def summed(array, axes):
    for axis in axes:
        step = 1
        while step < lax.axis_size(axis):
            array = array + crossed(array, axis, step)
            step *= 2
    return array


def select_rows(matrix, rows, dims):
    return lax.dot_general(matrix, rows, dims, preferred_element_type=f32).astype(bf16)


def matmul(left, right, dims=plain):
    return lax.dot_general(left, right, dims, preferred_element_type=f32)


def shards(
    tokens,
    lengths,
    order,
    mixer_gain,
    feed_gain,
    in_weight,
    conv_taps,
    out_weight,
    gate_up,
    down_weight,
    cotangent,
):
    local_rows = tokens.shape[1]
    seq_count, wt_count, grp_count = (lax.axis_size(a) for a in ("seq", "wt", "grp"))
    seq_at, wt_at, grp_at = (lax.axis_index(a) for a in ("seq", "wt", "grp"))
    peers = seq_count * wt_count
    per_peer = local_rows // peers
    block_index = seq_at * wt_count + wt_at
    places = [(a, b) for a in range(seq_count) for b in range(grp_count)]
    others = range(1, seq_count)
    steps = range(1, grp_count)
    ring = list(steps) + [0]
    shard_width = in_weight.shape[0]
    channels = out_weight.shape[0]
    half = gate_up.shape[2] // 2
    def relative(array):
        return relative_columns(array, seq_at, grp_at, seq_count, grp_count)
    stages = Sequence()
    by_seq, by_grp = Chain(stages, "seq", 2), Chain(stages, "grp", 2)
    backwards = [*others, 0]
    def grp_steps(held, sides=(0,)):
        for b in steps:
            for a in sides:
                held[(a, b)] = by_grp.send(held[(a, b - 1)], 1)
                yield
    def side_steps(held):
        moving = None
        for b in steps:
            if moving is None:
                moving = jnp.concatenate([held[(a, 0)] for a in range(seq_count)], axis=1)
            moving = by_grp.send(moving, 1)
            for a in range(seq_count):
                held[(a, b)] = block(moving, a, 1)
            yield
    def seq_steps(held, at=None):
        for b in [0, *steps] if at is None else at:
            for a in others:
                held[(a, b)] = by_seq.send(held[(0, b)], a)
            yield
    def gathering(values):
        step = wt_count // 2
        while step:
            got = stages.send(values, lambda v, step=step: crossed(v, "wt", step))
            yield
            values = jnp.concatenate([values, got], axis=0)
            step //= 2
        yield stages.tie(values)
    def scattering(sent, kept):
        step = 1
        while step < wt_count:
            got = stages.send(sent.astype(bf16), lambda v, step=step: crossed(v, "wt", step))
            yield
            total = kept + stages.tie(got).astype(f32)
            kept, sent = (total[: total.shape[0] // 2], total[total.shape[0] // 2 :])
            step *= 2
        yield total
    def halves(array, axis=0):
        return jnp.split(array, 2, axis=axis)
    def into_width(grads):
        return jnp.einsum("ktc,kdc->td", grads, full_in, preferred_element_type=f32)
    def side(array, a):
        return array[:, a * grp_count * shard_width : (a + 1) * grp_count * shard_width]
    def block(array, b, axis):
        return lax.slice_in_dim(array, b * shard_width, (b + 1) * shard_width, axis=axis)
    def whole(held, axis):
        return jnp.concatenate([held[p] for p in places], axis=axis)
    class Reduction:
        def __init__(self, axis):
            self.axis, self.came = axis, {}

        def part(self, a, b):
            return block(self.products[a], b, self.axis)

        def seq(self, size=1):
            for group in [ring[i : i + size] for i in range(0, grp_count, size)]:
                for a in others:
                    sent = [self.part(a, b) for b in group]
                    got = by_seq.send(
                        sent[0] if len(sent) == 1 else jnp.concatenate(sent, axis=self.axis), -a
                    )
                    for i, b in enumerate(group):
                        self.came[(a, b)] = block(got, i, self.axis)
                yield

        def summed(self, b):
            return sum(
                [self.came[(a, b)].astype(f32) for a in others], self.part(0, b).astype(f32)
            )

        def grp(self):
            self.total = self.summed(ring[0])
            for b in ring[1:]:
                got = by_grp.send(self.total.astype(bf16), 1)
                yield
                self.total = self.summed(b) + got.astype(f32)

        def grp_first(self):
            def both(b):
                return jnp.concatenate([self.part(a, b) for a in [0, *others]], axis=self.axis)

            self.totals = both(ring[0])
            for b in ring[1:]:
                got = by_grp.send(self.totals.astype(bf16), 1)
                yield
                self.totals = both(b).astype(f32) + got.astype(f32)

        def seq_last(self):
            self.total = block(self.totals, 0, self.axis)
            for a in others:
                got = by_seq.send(block(self.totals, a, self.axis).astype(bf16), -a)
                self.total = self.total + got.astype(f32)
    def producing(reduction, left, right):
        reduction.products = {}
        for a in backwards:
            if right.ndim == 3:
                product = jnp.einsum(
                    "td,ktc->kdc", stages.tie(side(left, a)), right, preferred_element_type=f32
                )
            elif reduction.axis == 0:
                product = matmul(stages.tie(side(left, a)), right, contract_rows)
            else:
                product = matmul(stages.tie(left), side(right, a), contract_rows)
            reduction.products[a] = stages.mark(product.astype(bf16))
            if a in (backwards[-2], backwards[-1]):
                yield
    def hidden_part(array, h):
        return array[..., h * half : (h + 1) * half]
    in_held = {(0, 0): in_weight.transpose(1, 0, 2)}
    out_held = {(0, 0): out_weight}
    gate_held = [
        {(0, 0): hidden_part(gate_up, h).reshape(shard_width, 2 * half)} for h in range(2)
    ]
    down_held = [{(0, 0): down_weight[h * half : (h + 1) * half]} for h in range(2)]
    in_grp, out_grp = grp_steps(in_held), grp_steps(out_held)
    gate_grp = [grp_steps(held) for held in gate_held]
    down_grp = [side_steps(held) for held in down_held]
    in_seq, out_seq = seq_steps(in_held), seq_steps(out_held)
    gate_seq = [seq_steps(held) for held in gate_held]
    down_seq = [seq_steps(held, [0]) for held in down_held]
    go(in_grp)
    by_seq.depth = 2
    go(in_seq)
    by_grp.depth = 2
    order_row = order[0]
    slot_blocks = order_row.reshape(peers, local_rows)
    here_positions = lax.dynamic_index_in_dim(slot_blocks, block_index, 0, keepdims=False)
    targets = here_positions // local_rows
    slots = jnp.arange(local_rows, dtype=jnp.int32)
    earlier = slots[:, None] < slots[None, :]
    same = (targets[:, None] == targets[None, :]) & earlier
    send_place = targets * per_peer + jnp.sum(same.astype(jnp.int32), axis=0)
    send_matrix = (slots[:, None] == send_place[None, :]).astype(bf16)
    mine = slot_blocks // local_rows == block_index
    mine_rank = matmul(mine.astype(bf16), earlier.astype(bf16)).astype(jnp.int32)
    sources = jnp.arange(peers, dtype=jnp.int32)
    arrival = jnp.where(mine, sources[:, None] * per_peer + mine_rank, -1).reshape(-1)
    home_place = order_row - block_index * local_rows
    home_hot = (home_place[:, None] == slots[None, :]).astype(bf16)
    arrival_hot = (arrival[:, None] == slots[None, :]).astype(bf16)
    def exchange(rows):
        return lax.all_to_all(rows, ("seq", "wt"), split_axis=0, concat_axis=0, tiled=True)
    by_grp.depth = 2
    tokens_got = stages.send(select_rows(send_matrix, tokens[0], plain), exchange)
    home_matrix = stages.mark(matmul(stages.tie(home_hot), arrival_hot, contract_rows).astype(bf16))
    cot_sent = stages.mark(select_rows(send_matrix, stages.tie(cotangent[0]), plain))
    def home_of(got):
        return relative(select_rows(home_matrix, stages.tie(got), plain))
    def to_arrival(rows):
        return stages.send(select_rows(home_matrix, relative(rows), contract_rows), exchange)
    def arrived(got):
        return select_rows(send_matrix, got, contract_rows)
    mixer_row = relative(mixer_gain[None])
    feed_row = relative(feed_gain[None])
    go(in_grp)
    token_rows = home_of(tokens_got).astype(f32)
    scale_mix = rms_scale(token_rows)
    go(in_seq)
    go(in_seq)
    go(in_grp)
    normed = gathering((token_rows * scale_mix * mixer_row).astype(bf16))
    next(normed)
    by_seq.depth = 2
    by_grp.depth = 2
    go(out_seq)
    go(out_grp)
    go(in_seq)
    go(out_grp)
    by_grp.depth = 3
    next(normed)
    normed_all = next(normed)
    go(out_seq)
    span_rows = normed_all.shape[0]
    go(out_grp)
    full_in = whole(in_held, 1)
    go(gate_grp[0])
    in_source = stages.tie(normed_all)
    in_gate, out_gate, values = (matmul(in_source, full_in[k]) for k in range(3))
    by_seq.depth = 2
    gated = stages.mark((in_gate * values).astype(bf16))
    rel = peer_order(wt_count)
    place_of = jnp.array([rel.index(j) for j in range(wt_count)] + [wt_count], dtype=jnp.int32)
    block_at = [wt_at ^ j for j in rel]
    def taken(array, at):
        return lax.dynamic_index_in_dim(array, at, 0, keepdims=False)
    def row_of(block):
        return place_of[wt_at ^ block]
    tails = gated.reshape(wt_count, local_rows, channels)[:, -2:]
    go(gate_grp[1])
    carried = stages.send(
        taken(tails, row_of(wt_count - 1)), lambda v: passed_along(v, "seq", 1)
    )
    tails = jnp.concatenate([tails, stages.tie(carried)[None]], axis=0)
    go(out_seq)
    by_grp.depth = 3
    go(out_seq)
    before = jnp.stack(
        [
            taken(tails, jnp.where(at == 0, wt_count, row_of(jnp.maximum(at - 1, 0))))
            for at in block_at
        ]
    )
    extended = jnp.concatenate(
        [before, gated.reshape(wt_count, local_rows, channels)], axis=1
    ).astype(f32)
    positions = (
        (seq_at * wt_count + jnp.stack(block_at))[:, None] * local_rows + slots[None, :]
    )[:, :, None]
    docs = lengths.shape[1]
    starts = [sum([lengths[0, i] for i in range(d)], jnp.int32(0)) for d in range(docs)]
    def mask(at, back):
        opening = jnp.zeros_like(at)
        for start in starts:
            opening = jnp.where(start <= at, jnp.maximum(opening, start), opening)
        return (at - back >= opening).astype(f32)
    mask_one, mask_two = mask(positions, 1), mask(positions, 2)
    taps = conv_taps.astype(f32)
    now, one_back, two_back = extended[:, 2:], extended[:, 1:-1], extended[:, :-2]
    mixed = (taps[2] * now + mask_one * taps[1] * one_back + mask_two * taps[0] * two_back).reshape(
        span_rows, channels
    )
    mixed_out = stages.mark((out_gate * mixed).astype(bf16))
    full_out = whole(out_held, 1)
    kept, sent = halves(stages.tie(mixed_out))
    go(gate_seq[0])
    by_grp.settle()
    kept = stages.mark(matmul(kept, full_out))
    sent = stages.mark(matmul(sent, full_out).astype(bf16))
    go(gate_seq[0])
    branch = scattering(sent, kept)
    go(gate_grp[0])
    next(branch)
    next(branch)
    go(gate_grp[1])
    go(down_seq[0])
    go(gate_seq[0])
    hidden_state = token_rows + next(branch)
    scale_feed = rms_scale(hidden_state)
    by_seq.settle()
    go(down_seq[1])
    feed = gathering((hidden_state * scale_feed * feed_row).astype(bf16))
    go(gate_grp[0])
    next(feed)
    go(gate_grp[1])
    cot_got = stages.send(cot_sent, exchange)
    by_grp.depth = 3
    by_grp.settle(2)
    go(gate_seq[0])
    next(feed)
    feed_all = next(feed)
    go(gate_seq[1])
    go(down_grp[0])
    cot_rows = home_of(cot_got)
    cot = gathering(cot_rows)
    go(gate_seq[1])
    by_grp.settle(2)
    by_grp.depth = 3
    next(cot)
    full_gate, gate_part, up_part, activated = ({} for _ in range(4))
    full_down, gates_grad = {}, {}
    def forward_half(h):
        full_gate[h] = whole(gate_held[h], 0)
        source = stages.tie(feed_all)
        gate_part[h] = matmul(source, full_gate[h][:, :half])
        up_part[h] = matmul(source, full_gate[h][:, half:])
        activated[h] = stages.mark(
            (gate_part[h] * jax.nn.sigmoid(gate_part[h]) * up_part[h]).astype(bf16)
        )
    forward_half(0)
    def backward_half(h):
        full_down[h] = whole(down_held[h], 1)
        act_grad = matmul(stages.tie(cot_all), full_down[h], contract_cols)
        gate, sigmoid_gate = gate_part[h], jax.nn.sigmoid(gate_part[h])
        gates_grad[h] = stages.mark(
            jnp.concatenate(
                [
                    (act_grad * up_part[h] * sigmoid_gate * (1.0 + gate * (1.0 - sigmoid_gate))).astype(
                        bf16
                    ),
                    (act_grad * gate * sigmoid_gate).astype(bf16),
                ],
                axis=1,
            )
        )
    gating, down = [Reduction(0), Reduction(0)], [Reduction(1), Reduction(1)]
    gating_seq, gating_grp = [g.seq() for g in gating], [g.grp() for g in gating]
    down_first, down_then = down[0].grp_first(), down[1].grp()
    down_swap = down[1].seq(2)
    next(cot)
    cot_all = next(cot)
    go(gate_seq[1])
    go(down_grp[0])
    go(down_grp[0])
    by_grp.settle(2)
    rest(producing(down[0], activated[0], cot_all))
    go(gate_seq[1])
    by_seq.settle(2)
    go(down_grp[1])
    go(down_grp[1])
    by_seq.settle(2)
    rest(down_grp[0])
    backward_half(0)
    go(down_grp[1])
    gating_work = producing(gating[0], feed_all, gates_grad[0])
    by_seq.settle(2)
    by_grp.depth = 3
    by_grp.depth = 3
    go(gating_work)
    go(gating_seq[0])
    go(gating_seq[0])
    rest(gate_seq[1])
    go(down_first)
    forward_half(1)
    rest(producing(down[1], activated[1], cot_all))
    by_grp.depth = 1
    go(down_swap)
    go(down_first)
    go(gating_seq[0])
    by_grp.depth = 1
    go(gating_work)
    rest(down_grp[1])
    backward_half(1)
    go(down_first)
    go(down_first)
    go(down_swap)
    go(gating_seq[0])
    gating_work = producing(gating[1], feed_all, gates_grad[1])
    by_grp.settle()
    go(gating_work)
    go(down_first)
    by_grp.depth = 3
    by_seq.settle()
    norm_grad = stages.mark(
        matmul(stages.tie(gates_grad[0]), full_gate[0], contract_cols)
    )
    go(gating_work)
    go(down_swap)
    norm_grad = stages.mark(
        norm_grad + matmul(stages.tie(gates_grad[1]), full_gate[1], contract_cols)
    )
    kept, sent = halves(norm_grad)
    feed_norm = scattering(sent, kept)
    go(down_swap)
    next(feed_norm)
    go(down_first)
    next(feed_norm)
    go(gating_seq[1])
    by_grp.settle(2)
    go(gating_grp[0])
    by_grp.settle()
    by_grp.settle(2)
    go(gating_seq[1])
    feed_norm_grad = next(feed_norm)
    by_grp.depth = 1
    feed_hat = hidden_state * scale_feed
    feed_term = jnp.sum(feed_norm_grad * feed_hat, axis=0)
    feed_scaled = feed_norm_grad * feed_row
    hidden_grad = cot_rows.astype(f32) + scale_feed * (
        feed_scaled - feed_hat * jnp.mean(feed_scaled * feed_hat, axis=-1, keepdims=True)
    )
    branch_back = gathering(hidden_grad.astype(bf16))
    by_grp.depth = 3
    go(gating_grp[0])
    by_grp.depth = 2
    next(branch_back)
    go(down_then)
    by_seq.settle(2)
    fed = stages.mark(matmul(stages.tie(activated[0]), full_down[0]))
    go(gating_grp[0])
    rest(gating_grp[0])
    fed = stages.mark(fed + matmul(stages.tie(activated[1]), full_down[1]))
    by_grp.settle()
    next(branch_back)
    branch_grad = next(branch_back)
    mixed_out_grad = matmul(stages.tie(branch_grad), full_out, contract_cols)
    kept, sent = halves(fed)
    feed_out = scattering(sent, kept)
    by_seq.settle()
    next(feed_out)
    out_gate_grad = (mixed_out_grad * mixed).astype(bf16)
    mixed_grad = stages.mark((mixed_out_grad * out_gate).astype(bf16))
    heads = mixed_grad.reshape(wt_count, local_rows, channels)[:, :2]
    by_seq.settle(2)
    incoming = stages.send(taken(heads, row_of(0)), lambda v: passed_along(v, "seq", -1))
    out_sum, in_sum = Reduction(1), Reduction(1)
    out_swap, out_ring = out_sum.seq(), out_sum.grp()
    in_swap, in_ring = in_sum.seq(), in_sum.grp()
    rest(producing(out_sum, mixed_out, branch_grad))
    next(feed_out)
    by_grp.depth = 2
    go(down_then)
    by_grp.depth = 2
    go(gating_seq[1])
    go(down_then)
    go(gating_seq[1])
    rest(down_then)
    by_seq.settle()
    go(gating_grp[1])
    heads = jnp.concatenate([heads, stages.tie(incoming)[None]], axis=0)
    last = wt_count - 1
    behind = jnp.stack(
        [
            taken(heads, jnp.where(at == last, wt_count, row_of(jnp.minimum(at + 1, last))))
            for at in block_at
        ]
    )
    grad_ext = jnp.concatenate(
        [mixed_grad.reshape(wt_count, local_rows, channels), behind], axis=1
    ).astype(f32)
    mixed_low = grad_ext[:, :-2]
    gated_grad = (
        taps[2] * mixed_low
        + taps[1] * mask(positions + 1, 1) * grad_ext[:, 1:-1]
        + taps[0] * mask(positions + 2, 2) * grad_ext[:, 2:]
    )
    taps_term = jnp.stack(
        [
            jnp.sum(mixed_low * mask_two * two_back, axis=(0, 1)),
            jnp.sum(mixed_low * mask_one * one_back, axis=(0, 1)),
            jnp.sum(mixed_low * now, axis=(0, 1)),
        ]
    )
    gated_low = gated_grad.astype(bf16).astype(f32).reshape(span_rows, channels)
    projected_grad = stages.mark(
        jnp.stack(
            [(gated_low * values).astype(bf16), out_gate_grad, (gated_low * in_gate).astype(bf16)]
        )
    )
    by_grp.depth = 2
    in_work = producing(in_sum, normed_all, projected_grad)
    kept, sent = halves(stages.tie(projected_grad), 1)
    by_seq.settle(2)
    by_seq.settle()
    by_grp.settle()
    go(out_swap)
    kept = stages.mark(into_width(kept))
    sent = stages.mark(into_width(sent).astype(bf16))
    by_grp.depth = 1
    mix_norm = scattering(sent, kept)
    next(mix_norm)
    go(gating_grp[1])
    go(in_work)
    next(mix_norm)
    go(out_swap)
    go(in_work)
    go(out_swap)
    go(out_swap)
    go(gating_grp[1])
    by_grp.settle(2)
    mix_norm_grad = next(mix_norm)
    block_got = to_arrival((hidden_state + next(feed_out)).astype(bf16))
    rest(gating_grp[1])
    mix_hat = token_rows * scale_mix
    mixer_term = jnp.sum(mix_norm_grad * mix_hat, axis=0)
    mix_scaled = mix_norm_grad * mixer_row
    grad_home = hidden_grad + scale_mix * (
        mix_scaled - mix_hat * jnp.mean(mix_scaled * mix_hat, axis=-1, keepdims=True)
    )
    go(out_ring)
    grad_got = to_arrival(grad_home.astype(bf16))
    down[0].seq_last()
    by_seq.settle()
    go(in_swap)
    go(out_ring)
    go(in_swap)
    go(in_swap)
    go(out_ring)
    by_seq.settle()
    rest(out_ring)
    block_out = arrived(block_got)
    gains = summed(relative(jnp.stack([mixer_term, feed_term])), ("wt", "seq", "grp"))
    taps_grad = summed(taps_term, ("seq", "grp"))
    tokens_grad = arrived(grad_got).astype(f32)
    go(in_ring)
    go(in_swap)
    go(in_ring)
    go(in_ring)
    rest(in_ring)
    out_grad = out_sum.total
    in_grad = in_sum.total.transpose(1, 0, 2)
    down_grad = jnp.concatenate([d.total for d in down], axis=0)
    gating_grad = jnp.concatenate(
        [g.total.reshape(shard_width, 2, half) for g in gating], axis=2
    )
    return (
        block_out[None],
        tokens_grad[None],
        gains[0],
        gains[1],
        in_grad,
        taps_grad,
        out_grad,
        gating_grad,
        down_grad,
    )


def solution(mesh):
    in_specs = (
        P("grp", ("seq", "wt"), None),
        P("grp", None),
        P("grp", None),
        P(),
        P(),
        P(("seq", "grp"), None, "wt"),
        P(None, "wt"),
        P("wt", ("seq", "grp")),
        P(("seq", "grp"), None, "wt"),
        P("wt", ("seq", "grp")),
        P("grp", ("seq", "wt"), None),
    )
    out_specs = (
        P("grp", ("seq", "wt"), None),
        P("grp", ("seq", "wt"), None),
        P(),
        P(),
        P(("seq", "grp"), None, "wt"),
        P(None, "wt"),
        P("wt", ("seq", "grp")),
        P(("seq", "grp"), None, "wt"),
        P("wt", ("seq", "grp")),
    )
    return jax.shard_map(shards, mesh=mesh, in_specs=in_specs, out_specs=out_specs, check_vma=False)
```
